256 devices in a mesh: section: 4 (over y), seq: 64 (over z, x, core).
Axes of the slice: x: 4, y: 4, z: 8, core: 2. Of those that a mesh axis runs over, the one named last changes fastest.
Arguments:
- span_inputs: bfloat16 [4, 2048, 3, 8192], P('section', 'seq'), may hold values from -28 to 28
- out_grad: bfloat16 [4, 2048, 8192], P('section', 'seq'), may hold values from -48 to 48
- past_cache: bfloat16 [4, 3072, 2, 64, 128], P('section', None, None, 'seq'), may hold values from -5 to 5
- past_accum: float32 [4, 3072, 2, 64, 128], P('section', None, None, 'seq'), may hold values from -0.6 to 0.6
- offsets: int32 [4], P('section'), may hold values from 0 to 3072, as said below
- lengths: int32 [4], P('section'), may hold values from 1024 to 2048, as said below
Outputs:
- next_grads: bfloat16 [4, 2048, 3, 8192], P('section', 'seq')
- new_accum: float32 [4, 3072, 2, 64, 128], P('section', None, None, 'seq')
The draws below stay inside these ranges and needn't reach their ends.
Inputs may be any that keep to these rules, and one draw needn't show every extreme that they name: The first offsets[s] rows of past_cache[s] and past_accum[s] belong to the sequence; one section's offset is 3072. Rows of a span from lengths[s] on are padding; one section's length is 2048.
All inputs are finite; a program needn't handle non-finite values.
Results may differ from the reference program's by a relative error of at most 0.0068.
Values may be sent and summed in bfloat16 or wider, within the bound.
No kernel may reach another device: no remote copies, remote signals or barrier semaphores. Data moves between devices by JAX's collectives and lax.ppermute only.
A program may use at most 128 MiB of HBM per device.

```python
import math
import jax
import jax.numpy as jnp
from jax import lax

HEADS = 64
DH = 128
D = 8192
SPAN = 2048
PAST = 3072
SECTIONS = 4


def draw_span_inputs(key, part):
    base_draw = jnp.clip(jax.random.normal(key, (SECTIONS, SPAN, 3, D), jnp.float32), -5.0, 5.0)
    return base_draw.astype(jnp.bfloat16)


def draw_offsets(key, part):
    first_key, pick_key = jax.random.split(jax.random.fold_in(key, 41))
    drawn = jax.random.randint(first_key, (SECTIONS,), 0, PAST + 1)
    return drawn.at[jax.random.randint(pick_key, (), 0, SECTIONS)].set(PAST).astype(jnp.int32)


def draw_lengths(key, part):
    first_key, pick_key = jax.random.split(jax.random.fold_in(key, 53))
    drawn = jax.random.randint(first_key, (SECTIONS,), SPAN // 2, SPAN + 1)
    return drawn.at[jax.random.randint(pick_key, (), 0, SECTIONS)].set(SPAN).astype(jnp.int32)


def shard_levels(own_key, extent, cuts, smallest, top_value):
    level = 1.0
    for position, parts in cuts:
        draws = jax.random.uniform(jax.random.fold_in(jax.random.fold_in(own_key, 6), position), (parts,), jnp.float32, smallest / len(cuts), top_value / len(cuts))
        level = level * jnp.repeat(jnp.exp(draws), extent[position] // parts).reshape((-1,) + (1,) * (len(extent) - 1 - position))
    return level


def scatter_about(stream_key, extent, width, limit, cuts=(), kind=jnp.bfloat16):
    values = jax.random.normal(stream_key, extent, jnp.float32) * width
    if len(cuts) > 0:
        values = shard_levels(stream_key, extent, cuts, -0.22, 0.18) * values
    return jnp.clip(values, min=-limit, max=limit).astype(kind)


def setup_inputs(seed: int = 0) -> dict:
    key_list = jax.random.split(jax.random.key(seed), 7)
    return {
        "span_inputs": draw_span_inputs(jax.random.fold_in(key_list[6], 71), 0),
        "out_grad": scatter_about(key_list[1], (SECTIONS, SPAN, D), 8.0, 48.0, ((0, 4), (1, 64))),
        "past_cache": scatter_about(key_list[2], (SECTIONS, PAST, 2, HEADS, DH), 1.0, 5.0, ((0, 4), (3, 64))),
        "past_accum": scatter_about(key_list[3], (SECTIONS, PAST, 2, HEADS, DH), 0.1, 0.6, ((0, 4), (3, 64)), jnp.float32),
        "offsets": draw_offsets(jax.random.fold_in(key_list[6], 71), 0),
        "lengths": draw_lengths(jax.random.fold_in(key_list[6], 71), 0),
    }


def head_grads(query_h, keys_h, values_h, dout_h, visible):
    scale_factor = 1.0 / math.sqrt(DH)
    raw_scores = jnp.dot(query_h, keys_h.T, preferred_element_type=jnp.float32) * scale_factor
    masked = jnp.where(visible, raw_scores, -jnp.inf)
    row_max = lax.optimization_barrier(jnp.max(masked, axis=-1, keepdims=True))
    exp_terms = jnp.exp(masked - row_max)
    attention = exp_terms / lax.optimization_barrier(jnp.sum(exp_terms, axis=-1, keepdims=True))
    attention_low = attention.astype(jnp.bfloat16)
    dprobs = jnp.dot(dout_h, values_h.T, preferred_element_type=jnp.float32)
    row_delta = lax.optimization_barrier(jnp.sum(attention * dprobs, axis=-1, keepdims=True))
    dscores = (attention * (dprobs - row_delta)).astype(jnp.bfloat16)
    grad_query = (jnp.dot(dscores, keys_h, preferred_element_type=jnp.float32) * scale_factor).astype(jnp.bfloat16)
    grad_keys = jnp.dot(dscores.T, query_h, preferred_element_type=jnp.float32) * scale_factor
    grad_values = jnp.dot(attention_low.T, dout_h, preferred_element_type=jnp.float32)
    return (grad_query, grad_keys, grad_values)

def section_grads(inputs_now, dout_now, cache_now, accum_now, offset, length):
    local_rows = inputs_now.reshape(SPAN, 3, HEADS, DH)
    positions = jnp.arange(SPAN, dtype=jnp.int32)
    dout_heads = jnp.where((positions < length)[:, None, None], dout_now.reshape(SPAN, HEADS, DH), jnp.zeros((), jnp.bfloat16))
    all_keys = jnp.concatenate([cache_now[:, 0], local_rows[:, 1]], axis=0)
    all_values = jnp.concatenate([cache_now[:, 1], local_rows[:, 2]], axis=0)
    key_index = jnp.arange(PAST + SPAN, dtype=jnp.int32)
    in_span = key_index - PAST
    visible = jnp.where(key_index[None, :] < PAST, key_index[None, :] < offset, (in_span[None, :] <= positions[:, None]) & (in_span[None, :] < length))

    def per_head(items):
        return head_grads(items[0], items[1], items[2], items[3], visible)
    grad_query, grad_keys, grad_values = lax.map(per_head, (jnp.transpose(local_rows[:, 0], (1, 0, 2)), jnp.transpose(all_keys, (1, 0, 2)), jnp.transpose(all_values, (1, 0, 2)), jnp.transpose(dout_heads, (1, 0, 2))))
    span_grads = jnp.stack([grad_query, grad_keys[:, PAST:].astype(jnp.bfloat16), grad_values[:, PAST:].astype(jnp.bfloat16)], axis=0)
    span_grads = jnp.transpose(span_grads, (2, 0, 1, 3)).reshape(SPAN, 3, D)
    added = jnp.transpose(jnp.stack([grad_keys[:, :PAST], grad_values[:, :PAST]], axis=0), (2, 0, 1, 3))
    return (span_grads, accum_now + added)

def reference(span_inputs, out_grad, past_cache, past_accum, offsets, lengths):
    grads_list = []
    accum_list = []
    for section_idx in range(SECTIONS):
        span_grads, accum_new = section_grads(span_inputs[section_idx], out_grad[section_idx], past_cache[section_idx], past_accum[section_idx], offsets[section_idx], lengths[section_idx])
        grads_list.append(span_grads)
        accum_list.append(accum_new)
    next_grads = jnp.roll(jnp.stack(grads_list, axis=0), -1, axis=0)
    return (next_grads, jnp.stack(accum_list, axis=0))
```

```python
import functools
import math

import jax
import jax.numpy as jnp
from jax import lax
from jax.experimental import pallas as pl
from jax.experimental.pallas import tpu as pltpu
from jax.sharding import PartitionSpec as P

HEADS = 64
DH = 128
NEG = -1e30
SCALE = 1.0 / math.sqrt(DH)
SCALE_LOG2 = SCALE * math.log2(math.e)
F32 = jnp.float32
BF16 = jnp.bfloat16
BQ = 512
BK = 1024
BS = 512


def pack_kernel(x_ref, g_ref, o_ref):
    for h in range(o_ref.shape[0]):
        cols = slice(h * DH, (h + 1) * DH)
        for p in range(3):
            o_ref[h, p] = x_ref[p, :, cols]
        o_ref[h, 3] = g_ref[:, cols]


def pack(x, g, heads_per_step=16):
    rows = x.shape[1]
    w = heads_per_step * DH
    return pl.pallas_call(
        pack_kernel,
        out_shape=jax.ShapeDtypeStruct((HEADS, 4, rows, DH), BF16),
        grid=(HEADS // heads_per_step,),
        in_specs=[
            pl.BlockSpec((3, rows, w), lambda i: (0, 0, i)),
            pl.BlockSpec((rows, w), lambda i: (0, i)),
        ],
        out_specs=pl.BlockSpec((heads_per_step, 4, rows, DH), lambda i: (i, 0, 0, 0)),
        name="pack",
    )(x, g)


def unpack_kernel(x_ref, o_ref):
    for h in range(x_ref.shape[0]):
        for p in range(x_ref.shape[1]):
            o_ref[p, :, h * DH : (h + 1) * DH] = x_ref[h, p]


def unpack(x, heads_per_step=16):
    planes, rows = x.shape[1], x.shape[2]
    return pl.pallas_call(
        unpack_kernel,
        out_shape=jax.ShapeDtypeStruct((planes, rows, HEADS * DH), BF16),
        grid=(HEADS // heads_per_step,),
        in_specs=[pl.BlockSpec((heads_per_step, planes, rows, DH), lambda i: (i, 0, 0, 0))],
        out_specs=pl.BlockSpec((planes, rows, heads_per_step * DH), lambda i: (0, 0, i)),
        name="unpack",
    )(x)


def attn_kernel(past, span, tok, sref, x_ref, pk_ref, pv_ref, acc_ref, og_ref, nacc_ref, s_sc, dp_sc, dka, dva):
    i = pl.program_id(0)
    nq = span // BQ
    offset = sref[0]
    length = sref[1]
    n_past = (offset + BK - 1) // BK

    @pl.when(i == 0)
    def _():
        dka[...] = jnp.zeros_like(dka)
        dva[...] = jnp.zeros_like(dva)

    def rows_of(plane, start, count):
        return x_ref[pl.ds(start // tok, count // tok), plane].reshape(count, DH)

    qstart = i * BQ
    dests = pl.ds(pl.multiple_of(qstart // tok, BQ // tok), BQ // tok)

    @pl.when(qstart >= length)
    def _():
        og_ref[dests, 0] = jnp.zeros((BQ // tok, tok, DH), BF16)

    @pl.when(qstart < length)
    def _():
        q = rows_of(0, qstart, BQ)
        g = rows_of(3, qstart, BQ)
        row = qstart + lax.broadcasted_iota(jnp.int32, (BQ, DH), 0)
        g = jnp.where(row < length, g, jnp.zeros_like(g))
        q_t = q.T
        g_t = g.T
        n_span = i + 1

        def fold(x, op):
            return op(x.reshape(x.shape[0] // 8, 8, BQ), axis=0)

        def score_past(b, m):
            r0 = pl.multiple_of(b * BK, BK)
            s = jnp.dot(pk_ref[pl.ds(r0, BK), :], q_t, preferred_element_type=F32)
            key = r0 + lax.broadcasted_iota(jnp.int32, (BK, BQ), 0)
            s = jnp.where(key < offset, s, NEG)
            s_sc[pl.ds(r0, BK), :] = s
            return jnp.maximum(m, fold(s, jnp.max))

        def score_span(b, m):
            r0 = pl.multiple_of(b * BS, BS)
            s = jnp.dot(rows_of(1, r0, BS), q_t, preferred_element_type=F32)
            key = r0 + lax.broadcasted_iota(jnp.int32, (BS, BQ), 0)
            query = qstart + lax.broadcasted_iota(jnp.int32, (BS, BQ), 1)
            s = jnp.where((key <= query) & (key < length), s, NEG)
            s_sc[pl.ds(pl.multiple_of(past + r0, BS), BS), :] = s
            return jnp.maximum(m, fold(s, jnp.max))

        m = lax.fori_loop(0, n_past, score_past, jnp.full((8, BQ), NEG, F32))
        m = lax.fori_loop(0, n_span, score_span, m)
        m_scaled = jnp.max(m, axis=0, keepdims=True) * SCALE_LOG2

        def stats(values, o0, size, carry):
            l, d = carry
            dp = jnp.dot(values, g_t, preferred_element_type=F32)
            e = jnp.exp2(s_sc[pl.ds(o0, size), :] * SCALE_LOG2 - m_scaled)
            s_sc[pl.ds(o0, size), :] = e
            dp_sc[pl.ds(o0, size), :] = dp
            return l + fold(e, jnp.sum), d + fold(e * dp, jnp.sum)

        def stats_past(b, carry):
            r0 = pl.multiple_of(b * BK, BK)
            return stats(pv_ref[pl.ds(r0, BK), :], r0, BK, carry)

        def stats_span(b, carry):
            r0 = pl.multiple_of(b * BS, BS)
            return stats(rows_of(2, r0, BS), pl.multiple_of(past + r0, BS), BS, carry)

        zero = jnp.zeros((8, BQ), F32)
        carry = lax.fori_loop(0, n_past, stats_past, (zero, zero))
        l, d = lax.fori_loop(0, n_span, stats_span, carry)
        inv_l = 1.0 / jnp.sum(l, axis=0, keepdims=True)
        delta = jnp.sum(d, axis=0, keepdims=True) * inv_l

        def grads(keys, o0, size, dq):
            p = s_sc[pl.ds(o0, size), :] * inv_l
            ds = (p * (dp_sc[pl.ds(o0, size), :] - delta)).astype(BF16)
            dva[pl.ds(o0, size), :] += jnp.dot(p.astype(BF16), g, preferred_element_type=F32)
            dka[pl.ds(o0, size), :] += jnp.dot(ds, q, preferred_element_type=F32)
            return dq + lax.dot_general(
                ds, keys, (((0,), (0,)), ((), ())), preferred_element_type=F32
            )

        def grads_past(b, dq):
            r0 = pl.multiple_of(b * BK, BK)
            return grads(pk_ref[pl.ds(r0, BK), :], r0, BK, dq)

        def grads_span(b, dq):
            r0 = pl.multiple_of(b * BS, BS)
            return grads(rows_of(1, r0, BS), pl.multiple_of(past + r0, BS), BS, dq)

        dq = lax.fori_loop(0, n_past, grads_past, jnp.zeros((BQ, DH), F32))
        dq = lax.fori_loop(0, n_span, grads_span, dq)
        og_ref[dests, 0] = (dq * SCALE).astype(BF16).reshape(BQ // tok, tok, DH)

    @pl.when(i == nq - 1)
    def _():
        n = span // tok
        og_ref[:, 1] = (dka[pl.ds(past, span), :] * SCALE).astype(BF16).reshape(n, tok, DH)
        og_ref[:, 2] = dva[pl.ds(past, span), :].astype(BF16).reshape(n, tok, DH)
        even = pl.ds(0, past, stride=2)
        odd = pl.ds(1, past, stride=2)
        nacc_ref[even, :] = acc_ref[even, :] + dka[pl.ds(0, past), :] * SCALE
        nacc_ref[odd, :] = acc_ref[odd, :] + dva[pl.ds(0, past), :]


def whole(shape):
    return pl.BlockSpec(shape, lambda i, s: (0,) * len(shape), pipeline_mode=pl.Buffered(1))


def attention_backward(bounds, x, past_k, past_v, accum):
    n, _, tok, _ = x.shape
    span, past = n * tok, past_k.shape[0]
    out_shape = (n, 3, tok, DH)
    return pl.pallas_call(
        functools.partial(attn_kernel, past, span, tok),
        out_shape=(jax.ShapeDtypeStruct(out_shape, BF16), jax.ShapeDtypeStruct(accum.shape, F32)),
        grid_spec=pltpu.PrefetchScalarGridSpec(
            num_scalar_prefetch=1,
            grid=(span // BQ,),
            in_specs=[whole(a.shape) for a in (x, past_k, past_v, accum)],
            out_specs=(whole(out_shape), whole(accum.shape)),
            scratch_shapes=[
                pltpu.VMEM((past + span, BQ), F32),
                pltpu.VMEM((past + span, BQ), F32),
                pltpu.VMEM((past + span, DH), F32),
                pltpu.VMEM((past + span, DH), F32),
            ],
        ),
        compiler_params=pltpu.CompilerParams(vmem_limit_bytes=56 * 2**20),
        name="attn_bwd",
    )(bounds, x, past_k, past_v, accum)


def from_behind(block, axis, distance):
    size = lax.axis_size(axis)
    return lax.ppermute(block, axis, [((i - distance) % size, i) for i in range(size)])


def per_device(span_inputs, out_grad, past_cache, past_accum, offsets, lengths):
    past = past_cache.shape[1]
    bounds = jnp.concatenate([offsets, lengths])
    packed = pack(jnp.transpose(span_inputs[0], (1, 0, 2)), out_grad[0])
    x = lax.all_to_all(packed, "seq", split_axis=0, concat_axis=0, tiled=True)
    cache = past_cache.reshape(past, 2, DH)
    grads, new_accum = attention_backward(
        bounds, x, cache[:, 0], cache[:, 1], past_accum.reshape(past * 2, DH)
    )
    y = lax.all_to_all(grads, "seq", split_axis=0, concat_axis=0, tiled=True)
    y = from_behind(y, "section", -1)
    out = jnp.transpose(unpack(y), (1, 0, 2))
    return out[None], new_accum.reshape(past_accum.shape)


def solution(mesh):
    in_specs = (
        P("section", "seq", None, None),
        P("section", "seq", None),
        P("section", None, None, "seq", None),
        P("section", None, None, "seq", None),
        P("section"),
        P("section"),
    )
    out_specs = (P("section", "seq", None, None), P("section", None, None, "seq", None))
    return jax.shard_map(
        per_device, mesh=mesh, in_specs=in_specs, out_specs=out_specs, check_vma=False
    )
```

```python
import functools
import math

import jax
import jax.numpy as jnp
from jax import lax
from jax.experimental import pallas as pl
from jax.experimental.pallas import tpu as pltpu
from jax.sharding import PartitionSpec as P

HEADS = 64
DH = 128
NEG = -1e30
SCALE = 1.0 / math.sqrt(DH)
SCALE_LOG2 = SCALE * math.log2(math.e)
F32 = jnp.float32
BF16 = jnp.bfloat16
BQ = 512
BK = 1024
MIB = 2**20


def pack_kernel(x_ref, g_ref, o_ref):
    for h in range(o_ref.shape[0]):
        cols = slice(h * DH, (h + 1) * DH)
        for p in range(3):
            o_ref[h, p] = x_ref[p, :, cols]
        o_ref[h, 3] = g_ref[:, cols]


def pack(x, g, heads_per_step=16):
    rows = x.shape[1]
    w = heads_per_step * DH
    return pl.pallas_call(
        pack_kernel,
        out_shape=jax.ShapeDtypeStruct((HEADS, 4, rows, DH), BF16),
        grid=(HEADS // heads_per_step,),
        in_specs=[
            pl.BlockSpec((3, rows, w), lambda i: (0, 0, i)),
            pl.BlockSpec((rows, w), lambda i: (0, i)),
        ],
        out_specs=pl.BlockSpec((heads_per_step, 4, rows, DH), lambda i: (i, 0, 0, 0)),
        compiler_params=pltpu.CompilerParams(vmem_limit_bytes=62 * MIB),
        name="pack",
    )(x, g)


def unpack_kernel(q_ref, kv_ref, o_ref):
    for h in range(q_ref.shape[0]):
        cols = slice(h * DH, (h + 1) * DH)
        o_ref[0, :, cols] = q_ref[h]
        o_ref[1, :, cols] = kv_ref[h, 0]
        o_ref[2, :, cols] = kv_ref[h, 1]


def unpack(q, kv, heads_per_step=16):
    rows = q.shape[1]
    return pl.pallas_call(
        unpack_kernel,
        out_shape=jax.ShapeDtypeStruct((3, rows, HEADS * DH), BF16),
        grid=(HEADS // heads_per_step,),
        in_specs=[
            pl.BlockSpec((heads_per_step, rows, DH), lambda i: (i, 0, 0)),
            pl.BlockSpec((heads_per_step, 2, rows, DH), lambda i: (i, 0, 0, 0)),
        ],
        out_specs=pl.BlockSpec((3, rows, heads_per_step * DH), lambda i: (0, 0, i)),
        compiler_params=pltpu.CompilerParams(vmem_limit_bytes=16 * MIB),
        name="unpack",
    )(q, kv)


def whole(shape):
    return pl.BlockSpec(shape, lambda i, s: (0,) * len(shape), pipeline_mode=pl.Buffered(1))


def dot(a, b):
    return jnp.dot(a, b, preferred_element_type=F32)


def dot_rows(a, b):
    return lax.dot_general(a, b, (((0,), (0,)), ((), ())), preferred_element_type=F32)


def token_rows(x_ref, plane, start, count):
    tok = x_ref.shape[2]
    return x_ref[pl.ds(start // tok, count // tok), plane].reshape(count, DH)


def live_rows(g, start, length):
    row = start + lax.broadcasted_iota(jnp.int32, g.shape, 0)
    return jnp.where(row < length, g, jnp.zeros_like(g))


def fold(x, op):
    return op(x.reshape(x.shape[0] // 8, 8, x.shape[1]), axis=0)


def mask_past(s, r0, offset):
    key = r0 + lax.broadcasted_iota(jnp.int32, s.shape, 0)
    return jnp.where(key < offset, s, NEG)


def span_kernel(bounds, x_ref, pk_ref, pv_ref, okv_ref, dq_ref, stat_ref, s_sc, dp_sc, dka, dva):
    n, _, tok, _ = x_ref.shape
    i = pl.program_id(0)
    offset = bounds[0]
    length = bounds[1]
    qstart = i * BQ

    @pl.when(i == 0)
    def _():
        dka[...] = jnp.zeros_like(dka)
        dva[...] = jnp.zeros_like(dva)

    @pl.when(qstart >= length)
    def _():
        dq_ref[...] = jnp.zeros_like(dq_ref)
        stat_ref[...] = jnp.zeros_like(stat_ref)

    @pl.when(qstart < length)
    def _():
        q = token_rows(x_ref, 0, qstart, BQ)
        g = live_rows(token_rows(x_ref, 3, qstart, BQ), qstart, length)
        q_t = q.T
        g_t = g.T
        half = BQ // 2
        lo = pl.ds(pl.multiple_of(qstart, BQ), half)
        hi = pl.ds(pl.multiple_of(qstart + half, half), half)

        def update(s, dp, carry):
            m, l, d = carry
            m_new = jnp.maximum(m, jnp.max(fold(s, jnp.max), axis=0, keepdims=True))
            keep = jnp.exp2((m - m_new) * SCALE_LOG2)
            e = jnp.exp2(s * SCALE_LOG2 - m_new * SCALE_LOG2)
            return m_new, l * keep + fold(e, jnp.sum), d * keep + fold(e * dp, jnp.sum)

        def past_stats(b, carry, masked):
            r0 = pl.multiple_of(b * BK, BK)
            size = BK // 2
            parts = [pl.ds(r0 + k * size, size) for k in range(2)]
            s = [dot(pk_ref[r, :], q_t) for r in parts]
            dp = [dot(pv_ref[r, :], g_t) for r in parts]
            for k in range(2):
                if masked:
                    s[k] = mask_past(s[k], r0 + k * size, offset)
                carry = update(s[k], dp[k], carry)
            return carry

        def span_stats(b, carry):
            r0 = pl.multiple_of(b * BQ, BQ)
            s = dot(token_rows(x_ref, 1, r0, BQ), q_t)
            dp = dot(token_rows(x_ref, 2, r0, BQ), g_t)
            s_sc[pl.ds(r0, BQ), :] = s
            dp_sc[pl.ds(r0, BQ), :] = dp
            return update(s, dp, carry)

        def diagonal_stats(carry):
            key = lax.broadcasted_iota(jnp.int32, (half, BQ), 0)
            query = lax.broadcasted_iota(jnp.int32, (half, BQ), 1)
            s = dot(token_rows(x_ref, 1, qstart, half), q_t)
            dp = dot(token_rows(x_ref, 2, qstart, half), g_t)
            s_hi = dot(token_rows(x_ref, 1, qstart + half, half), q_t[:, half:])
            dp_hi = dot(token_rows(x_ref, 2, qstart + half, half), g_t[:, half:])
            s = jnp.where((key <= query) & (qstart + key < length), s, NEG)
            s_sc[lo, :] = s
            dp_sc[lo, :] = dp
            carry = update(s, dp, carry)
            key = key[:, :half]
            seen = (key <= query[:, :half]) & (qstart + half + key < length)
            s_hi = jnp.where(seen, s_hi, NEG)
            s_sc[hi, half:] = s_hi
            dp_sc[hi, half:] = dp_hi
            right = update(s_hi, dp_hi, tuple(c[:, half:] for c in carry))
            return tuple(jnp.concatenate([c[:, :half], r], axis=1) for c, r in zip(carry, right))

        zero = jnp.zeros((8, BQ), F32)
        carry = (jnp.full((1, BQ), NEG, F32), zero, zero)
        carry = lax.fori_loop(0, i, span_stats, carry)
        carry = diagonal_stats(carry)
        full = offset // BK
        carry = lax.fori_loop(0, full, functools.partial(past_stats, masked=False), carry)
        m, l, d = lax.fori_loop(
            full, (offset + BK - 1) // BK, functools.partial(past_stats, masked=True), carry
        )
        l = jnp.sum(l, axis=0, keepdims=True)
        delta = jnp.sum(d, axis=0, keepdims=True) / l
        lse = m * SCALE_LOG2 + jnp.log2(l)
        stat_ref[...] = jnp.concatenate([lse, delta, jnp.zeros((6, BQ), F32)], axis=0)

        def p_and_ds(rows, cols):
            p = jnp.exp2(s_sc[rows, cols] * SCALE_LOG2 - lse[:, cols])
            return p.astype(BF16), (p * (dp_sc[rows, cols] - delta[:, cols])).astype(BF16)

        def span_grads(b, dq):
            rows = pl.ds(pl.multiple_of(b * BQ, BQ), BQ)
            p, ds = p_and_ds(rows, slice(0, BQ))
            dva[rows, :] += dot(p, g)
            dka[rows, :] += dot(ds, q)
            return dq + dot_rows(ds, token_rows(x_ref, 1, b * BQ, BQ))

        dq = lax.fori_loop(0, i, span_grads, jnp.zeros((BQ, DH), F32))
        p, ds = p_and_ds(lo, slice(0, BQ))
        p_hi, ds_hi = p_and_ds(hi, slice(half, BQ))
        dva[lo, :] += dot(p, g)
        dka[lo, :] += dot(ds, q)
        dva[hi, :] += dot(p_hi, g[half:])
        dka[hi, :] += dot(ds_hi, q[half:])
        dq = dq + dot_rows(ds, token_rows(x_ref, 1, qstart, half))
        dq_ref[:half] = dq[:half]
        dq_ref[half:] = dq[half:] + dot_rows(ds_hi, token_rows(x_ref, 1, qstart + half, half))

    @pl.when(i == pl.num_programs(0) - 1)
    def _():
        okv_ref[:, 0] = (dka[...] * SCALE).astype(BF16).reshape(n, tok, DH)
        okv_ref[:, 1] = dva[...].astype(BF16).reshape(n, tok, DH)


def span_grads_and_stats(bounds, x, pk, pv):
    n, _, tok, _ = x.shape
    span = n * tok
    return pl.pallas_call(
        span_kernel,
        out_shape=(
            jax.ShapeDtypeStruct((n, 2, tok, DH), BF16),
            jax.ShapeDtypeStruct((span, DH), F32),
            jax.ShapeDtypeStruct((8, span), F32),
        ),
        grid_spec=pltpu.PrefetchScalarGridSpec(
            num_scalar_prefetch=1,
            grid=(span // BQ,),
            in_specs=[whole(a.shape) for a in (x, pk, pv)],
            out_specs=(
                whole((n, 2, tok, DH)),
                pl.BlockSpec((BQ, DH), lambda i, s: (i, 0)),
                pl.BlockSpec((8, BQ), lambda i, s: (0, i)),
            ),
            scratch_shapes=[
                pltpu.VMEM((span, BQ), F32),
                pltpu.VMEM((span, BQ), F32),
                pltpu.VMEM((span, DH), F32),
                pltpu.VMEM((span, DH), F32),
            ],
        ),
        compiler_params=pltpu.CompilerParams(vmem_limit_bytes=62 * MIB),
        cost_estimate=pl.CostEstimate(flops=7 * 10**9, bytes_accessed=6 * 10**6, transcendentals=10**7),
        name="attn_span",
    )(bounds, x, pk, pv)


def query_kernel(bounds, x_ref, pk_ref, pv_ref, dqs_ref, stat_ref, o_ref):
    tok = x_ref.shape[2]
    offset = bounds[0]
    length = bounds[1]
    qstart = pl.program_id(0) * BQ

    @pl.when(qstart >= length)
    def _():
        o_ref[...] = jnp.zeros_like(o_ref)

    @pl.when(qstart < length)
    def _():
        q_t = token_rows(x_ref, 0, qstart, BQ).T
        g_t = live_rows(token_rows(x_ref, 3, qstart, BQ), qstart, length).T
        lse = stat_ref[0:1]
        delta = stat_ref[1:2]

        def step(b, dq):
            r0 = pl.multiple_of(b * BK, BK)
            keys = pk_ref[pl.ds(r0, BK), :]
            p = jnp.exp2(mask_past(dot(keys, q_t), r0, offset) * SCALE_LOG2 - lse)
            dp = dot(pv_ref[pl.ds(r0, BK), :], g_t)
            ds = (p * (dp - delta)).astype(BF16)
            return dq + dot_rows(ds, keys)

        dq = lax.fori_loop(0, (offset + BK - 1) // BK, step, dqs_ref[...])
        o_ref[...] = (dq * SCALE).astype(BF16).reshape(BQ // tok, tok, DH)


def query_grads(bounds, x, pk, pv, dq_span, stats):
    n, _, tok, _ = x.shape
    span = n * tok
    return pl.pallas_call(
        query_kernel,
        out_shape=jax.ShapeDtypeStruct((n, tok, DH), BF16),
        grid_spec=pltpu.PrefetchScalarGridSpec(
            num_scalar_prefetch=1,
            grid=(span // BQ,),
            in_specs=[whole(a.shape) for a in (x, pk, pv)]
            + [
                pl.BlockSpec((BQ, DH), lambda i, s: (i, 0)),
                pl.BlockSpec((8, BQ), lambda i, s: (0, i)),
            ],
            out_specs=pl.BlockSpec((BQ // tok, tok, DH), lambda i, s: (i, 0, 0)),
        ),
        compiler_params=pltpu.CompilerParams(vmem_limit_bytes=62 * MIB),
        cost_estimate=pl.CostEstimate(flops=5 * 10**9, bytes_accessed=6 * 10**6, transcendentals=10**7),
        name="attn_query",
    )(bounds, x, pk, pv, dq_span, stats)


def past_kernel(first, bounds, x_ref, pk_ref, pv_ref, stat_ref, acc_ref, prev_ref, nacc_ref, dk, dv):
    del prev_ref
    offset = bounds[0]
    length = bounds[1]
    kstart = (first + pl.program_id(0)) * BK
    dk[...] = jnp.zeros_like(dk)
    dv[...] = jnp.zeros_like(dv)

    def step(i, carry):
        qstart = pl.multiple_of(i * BQ, BQ)
        q = token_rows(x_ref, 0, qstart, BQ)
        g = live_rows(token_rows(x_ref, 3, qstart, BQ), qstart, length)
        s = mask_past(dot(pk_ref[...], q.T), kstart, offset)
        p = jnp.exp2(s * SCALE_LOG2 - stat_ref[0:1, pl.ds(qstart, BQ)])
        dp = dot(pv_ref[...], g.T)
        ds = (p * (dp - stat_ref[1:2, pl.ds(qstart, BQ)])).astype(BF16)
        dk[...] += dot(ds, q)
        dv[...] += dot(p.astype(BF16), g)
        return carry

    @pl.when(kstart < offset)
    def _():
        lax.fori_loop(0, (length + BQ - 1) // BQ, step, 0)

    even = pl.ds(0, BK, stride=2)
    odd = pl.ds(1, BK, stride=2)
    nacc_ref[even, :] = acc_ref[even, :] + dk[...] * SCALE
    nacc_ref[odd, :] = acc_ref[odd, :] + dv[...]


def past_grads(bounds, x, pk, pv, stats, accum, first, count, prev=None):
    keys = pl.BlockSpec((BK, DH), lambda i, s: (first + i, 0))
    pairs = pl.BlockSpec((2 * BK, DH), lambda i, s: (first + i, 0))
    args = [bounds, x, pk, pv, stats, accum]
    in_specs = [whole(x.shape), keys, keys, whole(stats.shape), pairs]
    body = functools.partial(past_kernel, first)
    aliases = {}
    if prev is None:
        body = lambda *refs: past_kernel(first, *refs[:6], None, *refs[6:])
    else:
        args.append(prev)
        in_specs.append(pl.BlockSpec(memory_space=pl.ANY))
        aliases = {6: 0}
    return pl.pallas_call(
        body,
        out_shape=jax.ShapeDtypeStruct(accum.shape, F32),
        grid_spec=pltpu.PrefetchScalarGridSpec(
            num_scalar_prefetch=1,
            grid=(count,),
            in_specs=in_specs,
            out_specs=pairs,
            scratch_shapes=[pltpu.VMEM((BK, DH), F32), pltpu.VMEM((BK, DH), F32)],
        ),
        input_output_aliases=aliases,
        compiler_params=pltpu.CompilerParams(vmem_limit_bytes=62 * MIB),
        cost_estimate=pl.CostEstimate(
            flops=2 * 10**9 * count, bytes_accessed=4 * 10**6 * count, transcendentals=10**6 * count
        ),
        name=f"attn_past{first}",
    )(*args)


def to_heads(x):
    return lax.all_to_all(x, "seq", split_axis=0, concat_axis=0, tiled=True)


def from_behind(block, axis, distance):
    size = lax.axis_size(axis)
    return lax.ppermute(block, axis, [((i - distance) % size, i) for i in range(size)])


def per_device(span_inputs, out_grad, past_cache, past_accum, offsets, lengths):
    past = past_cache.shape[1]
    bounds = jnp.concatenate([offsets, lengths])
    cache = past_cache.reshape(past, 2, DH)
    pk, pv = cache[:, 0], cache[:, 1]
    x = to_heads(pack(jnp.transpose(span_inputs[0], (1, 0, 2)), out_grad[0]))
    kv, dq_span, stats = span_grads_and_stats(bounds, x, pk, pv)
    kv = to_heads(kv)
    dq = query_grads(bounds, x, pk, pv, dq_span, stats)
    dq, bounds = lax.optimization_barrier((dq, bounds))
    dq = from_behind(dq, "section", -1)
    accum = past_accum.reshape(past * 2, DH)
    new_accum = past_grads(bounds, x, pk, pv, stats, accum, 0, 1)
    kv, dq, new_accum, bounds = lax.optimization_barrier((kv, dq, new_accum, bounds))
    dq = to_heads(dq)
    kv = from_behind(kv, "section", -1)
    new_accum = past_grads(bounds, x, pk, pv, stats, accum, 1, past // BK - 1, new_accum)
    out = jnp.transpose(unpack(dq, kv), (1, 0, 2))
    return out[None], new_accum.reshape(past_accum.shape)


def solution(mesh):
    in_specs = (
        P("section", "seq", None, None),
        P("section", "seq", None),
        P("section", None, None, "seq", None),
        P("section", None, None, "seq", None),
        P("section"),
        P("section"),
    )
    out_specs = (P("section", "seq", None, None), P("section", None, None, "seq", None))
    return jax.shard_map(
        per_device, mesh=mesh, in_specs=in_specs, out_specs=out_specs, check_vma=False
    )
```

```python
import functools
import math

import jax
import jax.numpy as jnp
from jax import lax
from jax.experimental import pallas as pl
from jax.experimental.pallas import tpu as pltpu
from jax.sharding import PartitionSpec as P

HEADS = 64
DH = 128
NEG = -1e30
SCALE = 1.0 / math.sqrt(DH)
SCALE_LOG2 = SCALE * math.log2(math.e)
F32 = jnp.float32
BF16 = jnp.bfloat16
BQ = 512
BK = 1024
MIB = 2**20


def pack_kernel(chunks, x_hbm, g_hbm, o_hbm, x_ref, g_ref, o_ref, in_sem, out_sem):
    heads = HEADS // chunks
    copies = []
    for c in range(chunks):
        cols = pl.ds(c * heads * DH, heads * DH)
        copies.append((
            pltpu.make_async_copy(x_hbm.at[:, :, cols], x_ref.at[:, :, cols], in_sem.at[0, c]),
            pltpu.make_async_copy(g_hbm.at[:, cols], g_ref.at[:, cols], in_sem.at[1, c]),
        ))
    for pair in copies:
        for copy in pair:
            copy.start()
    stores = []
    for c in range(chunks):
        for copy in copies[c]:
            copy.wait()
        for h in range(c * heads, (c + 1) * heads):
            cols = slice(h * DH, (h + 1) * DH)
            for p in range(3):
                o_ref[h, p] = x_ref[p, :, cols]
            o_ref[h, 3] = g_ref[:, cols]
        rows = pl.ds(c * heads, heads)
        stores.append(pltpu.make_async_copy(o_ref.at[rows], o_hbm.at[rows], out_sem.at[c]))
        stores[-1].start()
    for store in stores:
        store.wait()


def pack(x, g, chunks=8):
    shape = (HEADS, 4, x.shape[1], DH)
    hbm = pl.BlockSpec(memory_space=pl.ANY)
    return pl.pallas_call(
        functools.partial(pack_kernel, chunks),
        out_shape=jax.ShapeDtypeStruct(shape, BF16),
        in_specs=[hbm, hbm],
        out_specs=hbm,
        scratch_shapes=[
            pltpu.VMEM(x.shape, BF16),
            pltpu.VMEM(g.shape, BF16),
            pltpu.VMEM(shape, BF16),
            pltpu.SemaphoreType.DMA((2, chunks)),
            pltpu.SemaphoreType.DMA((chunks,)),
        ],
        compiler_params=pltpu.CompilerParams(vmem_limit_bytes=62 * MIB),
        name="pack",
    )(x, g)


def unpack_kernel(q_ref, kv_ref, o_ref):
    for h in range(q_ref.shape[0]):
        cols = slice(h * DH, (h + 1) * DH)
        o_ref[0, :, cols] = q_ref[h]
        o_ref[1, :, cols] = kv_ref[h, 0]
        o_ref[2, :, cols] = kv_ref[h, 1]


def unpack(q, kv, heads_per_step=16):
    rows = q.shape[1]
    return pl.pallas_call(
        unpack_kernel,
        out_shape=jax.ShapeDtypeStruct((3, rows, HEADS * DH), BF16),
        grid=(HEADS // heads_per_step,),
        in_specs=[
            pl.BlockSpec((heads_per_step, rows, DH), lambda i: (i, 0, 0)),
            pl.BlockSpec((heads_per_step, 2, rows, DH), lambda i: (i, 0, 0, 0)),
        ],
        out_specs=pl.BlockSpec((3, rows, heads_per_step * DH), lambda i: (0, 0, i)),
        compiler_params=pltpu.CompilerParams(vmem_limit_bytes=16 * MIB),
        name="unpack",
    )(q, kv)


def whole(shape):
    return pl.BlockSpec(shape, lambda i, s: (0,) * len(shape), pipeline_mode=pl.Buffered(1))


def dot(a, b):
    return jnp.dot(a, b, preferred_element_type=F32)


def dot_rows(a, b):
    return lax.dot_general(a, b, (((0,), (0,)), ((), ())), preferred_element_type=F32)


def token_rows(x_ref, plane, start, count):
    tok = x_ref.shape[2]
    return x_ref[pl.ds(start // tok, count // tok), plane].reshape(count, DH)


def live_rows(g, start, length):
    row = start + lax.broadcasted_iota(jnp.int32, g.shape, 0)
    return jnp.where(row < length, g, jnp.zeros_like(g))


def fold(x, op):
    return op(x.reshape(x.shape[0] // 8, 8, x.shape[1]), axis=0)


def mask_past(s, r0, offset):
    key = r0 + lax.broadcasted_iota(jnp.int32, s.shape, 0)
    return jnp.where(key < offset, s, NEG)


def past_copies(pk_hbm, pv_hbm, pk_ref, pv_ref, sems, b):
    rows = pl.ds(pl.multiple_of(b * BK, BK), BK)
    return (
        pltpu.make_async_copy(pk_hbm.at[rows], pk_ref.at[rows], sems.at[0, b]),
        pltpu.make_async_copy(pv_hbm.at[rows], pv_ref.at[rows], sems.at[1, b]),
    )


def each(count, action):
    def body(b, carry):
        action(b)
        return carry

    lax.fori_loop(0, count, body, 0)


def span_kernel(
    bounds, x_hbm, pk_hbm, pv_hbm, okv_ref, dq_ref, stat_ref,
    x_ref, pk_ref, pv_ref, s_sc, dp_sc, dka, dva, x_sem, past_sem,
):
    n, _, tok, _ = x_ref.shape
    i = pl.program_id(0)
    offset = bounds[0]
    length = bounds[1]
    qstart = i * BQ
    n_past = (offset + BK - 1) // BK

    def x_copy(c):
        rows = pl.ds(c * (BQ // tok), BQ // tok)
        return pltpu.make_async_copy(x_hbm.at[rows], x_ref.at[rows], x_sem.at[c])

    def start_past(b):
        for copy in past_copies(pk_hbm, pv_hbm, pk_ref, pv_ref, past_sem, b):
            copy.start()

    def wait_past(b):
        @pl.when(i == 0)
        def _():
            for copy in past_copies(pk_hbm, pv_hbm, pk_ref, pv_ref, past_sem, b):
                copy.wait()

    @pl.when(i == 0)
    def _():
        x_copy(0).start()
        each(n_past, start_past)
        for c in range(1, n * tok // BQ):
            x_copy(c).start()

    @pl.when(i == 0)
    def _():
        dka[...] = jnp.zeros_like(dka)
        dva[...] = jnp.zeros_like(dva)

    x_copy(i).wait()

    @pl.when(qstart >= length)
    def _():
        dq_ref[...] = jnp.zeros_like(dq_ref)
        stat_ref[...] = jnp.zeros_like(stat_ref)
        each(n_past, wait_past)

    @pl.when(qstart < length)
    def _():
        q = token_rows(x_ref, 0, qstart, BQ)
        g = live_rows(token_rows(x_ref, 3, qstart, BQ), qstart, length)
        q_t = q.T
        g_t = g.T
        half = BQ // 2
        lo = pl.ds(pl.multiple_of(qstart, BQ), half)
        hi = pl.ds(pl.multiple_of(qstart + half, half), half)

        def update(s, dp, carry):
            m, l, d = carry
            m_new = jnp.maximum(m, jnp.max(fold(s, jnp.max), axis=0, keepdims=True))
            keep = jnp.exp2((m - m_new) * SCALE_LOG2)
            e = jnp.exp2(s * SCALE_LOG2 - m_new * SCALE_LOG2)
            return m_new, l * keep + fold(e, jnp.sum), d * keep + fold(e * dp, jnp.sum)

        def past_stats(b, carry, masked):
            wait_past(b)
            r0 = pl.multiple_of(b * BK, BK)
            size = BK // 2
            parts = [pl.ds(r0 + k * size, size) for k in range(2)]
            s = [dot(pk_ref[r, :], q_t) for r in parts]
            dp = [dot(pv_ref[r, :], g_t) for r in parts]
            for k in range(2):
                if masked:
                    s[k] = mask_past(s[k], r0 + k * size, offset)
                carry = update(s[k], dp[k], carry)
            return carry

        def span_stats(b, carry):
            r0 = pl.multiple_of(b * BQ, BQ)
            s = dot(token_rows(x_ref, 1, r0, BQ), q_t)
            dp = dot(token_rows(x_ref, 2, r0, BQ), g_t)
            s_sc[pl.ds(r0, BQ), :] = s
            dp_sc[pl.ds(r0, BQ), :] = dp
            return update(s, dp, carry)

        def diagonal_stats(carry):
            key = lax.broadcasted_iota(jnp.int32, (half, BQ), 0)
            query = lax.broadcasted_iota(jnp.int32, (half, BQ), 1)
            s = dot(token_rows(x_ref, 1, qstart, half), q_t)
            dp = dot(token_rows(x_ref, 2, qstart, half), g_t)
            s_hi = dot(token_rows(x_ref, 1, qstart + half, half), q_t[:, half:])
            dp_hi = dot(token_rows(x_ref, 2, qstart + half, half), g_t[:, half:])
            s = jnp.where((key <= query) & (qstart + key < length), s, NEG)
            s_sc[lo, :] = s
            dp_sc[lo, :] = dp
            carry = update(s, dp, carry)
            key = key[:, :half]
            seen = (key <= query[:, :half]) & (qstart + half + key < length)
            s_hi = jnp.where(seen, s_hi, NEG)
            s_sc[hi, half:] = s_hi
            dp_sc[hi, half:] = dp_hi
            right = update(s_hi, dp_hi, tuple(c[:, half:] for c in carry))
            return tuple(jnp.concatenate([c[:, :half], r], axis=1) for c, r in zip(carry, right))

        zero = jnp.zeros((8, BQ), F32)
        carry = (jnp.full((1, BQ), NEG, F32), zero, zero)
        carry = lax.fori_loop(0, i, span_stats, carry)
        carry = diagonal_stats(carry)
        full = offset // BK
        carry = lax.fori_loop(0, full, functools.partial(past_stats, masked=False), carry)
        m, l, d = lax.fori_loop(
            full, n_past, functools.partial(past_stats, masked=True), carry
        )
        l = jnp.sum(l, axis=0, keepdims=True)
        delta = jnp.sum(d, axis=0, keepdims=True) / l
        lse = m * SCALE_LOG2 + jnp.log2(l)
        stat_ref[...] = jnp.concatenate([lse, delta, jnp.zeros((6, BQ), F32)], axis=0)

        def p_and_ds(rows, cols):
            p = jnp.exp2(s_sc[rows, cols] * SCALE_LOG2 - lse[:, cols])
            return p.astype(BF16), (p * (dp_sc[rows, cols] - delta[:, cols])).astype(BF16)

        def span_grads(b, dq):
            rows = pl.ds(pl.multiple_of(b * BQ, BQ), BQ)
            p, ds = p_and_ds(rows, slice(0, BQ))
            dva[rows, :] += dot(p, g)
            dka[rows, :] += dot(ds, q)
            return dq + dot_rows(ds, token_rows(x_ref, 1, b * BQ, BQ))

        dq = lax.fori_loop(0, i, span_grads, jnp.zeros((BQ, DH), F32))
        p, ds = p_and_ds(lo, slice(0, BQ))
        p_hi, ds_hi = p_and_ds(hi, slice(half, BQ))
        dva[lo, :] += dot(p, g)
        dka[lo, :] += dot(ds, q)
        dva[hi, :] += dot(p_hi, g[half:])
        dka[hi, :] += dot(ds_hi, q[half:])
        dq = dq + dot_rows(ds, token_rows(x_ref, 1, qstart, half))
        dq_ref[:half] = dq[:half]
        dq_ref[half:] = dq[half:] + dot_rows(ds_hi, token_rows(x_ref, 1, qstart + half, half))

    @pl.when(i == pl.num_programs(0) - 1)
    def _():
        okv_ref[:, 0] = (dka[...] * SCALE).astype(BF16).reshape(n, tok, DH)
        okv_ref[:, 1] = dva[...].astype(BF16).reshape(n, tok, DH)


def span_grads_and_stats(bounds, x, pk, pv):
    n, _, tok, _ = x.shape
    span = n * tok
    return pl.pallas_call(
        span_kernel,
        out_shape=(
            jax.ShapeDtypeStruct((n, 2, tok, DH), BF16),
            jax.ShapeDtypeStruct((span, DH), F32),
            jax.ShapeDtypeStruct((8, span), F32),
        ),
        grid_spec=pltpu.PrefetchScalarGridSpec(
            num_scalar_prefetch=1,
            grid=(span // BQ,),
            in_specs=[pl.BlockSpec(memory_space=pl.ANY)] * 3,
            out_specs=(
                whole((n, 2, tok, DH)),
                pl.BlockSpec((BQ, DH), lambda i, s: (i, 0)),
                pl.BlockSpec((8, BQ), lambda i, s: (0, i)),
            ),
            scratch_shapes=[
                pltpu.VMEM(x.shape, BF16),
                pltpu.VMEM(pk.shape, BF16),
                pltpu.VMEM(pv.shape, BF16),
                pltpu.VMEM((span, BQ), F32),
                pltpu.VMEM((span, BQ), F32),
                pltpu.VMEM((span, DH), F32),
                pltpu.VMEM((span, DH), F32),
                pltpu.SemaphoreType.DMA((span // BQ,)),
                pltpu.SemaphoreType.DMA((2, pk.shape[0] // BK)),
            ],
        ),
        compiler_params=pltpu.CompilerParams(vmem_limit_bytes=62 * MIB),
        cost_estimate=pl.CostEstimate(flops=7 * 10**9, bytes_accessed=6 * 10**6, transcendentals=10**7),
        name="attn_span",
    )(bounds, x, pk, pv)


def query_kernel(bounds, x_ref, pk_ref, pv_ref, dqs_ref, stat_ref, o_ref):
    tok = x_ref.shape[2]
    offset = bounds[0]
    length = bounds[1]
    qstart = pl.program_id(0) * BQ

    @pl.when(qstart >= length)
    def _():
        o_ref[...] = jnp.zeros_like(o_ref)

    @pl.when(qstart < length)
    def _():
        q_t = token_rows(x_ref, 0, qstart, BQ).T
        g_t = live_rows(token_rows(x_ref, 3, qstart, BQ), qstart, length).T
        lse = stat_ref[0:1]
        delta = stat_ref[1:2]

        def step(b, dq):
            r0 = pl.multiple_of(b * BK, BK)
            keys = pk_ref[pl.ds(r0, BK), :]
            p = jnp.exp2(mask_past(dot(keys, q_t), r0, offset) * SCALE_LOG2 - lse)
            dp = dot(pv_ref[pl.ds(r0, BK), :], g_t)
            ds = (p * (dp - delta)).astype(BF16)
            return dq + dot_rows(ds, keys)

        dq = lax.fori_loop(0, (offset + BK - 1) // BK, step, dqs_ref[...])
        o_ref[...] = (dq * SCALE).astype(BF16).reshape(BQ // tok, tok, DH)


def query_grads(bounds, x, pk, pv, dq_span, stats):
    n, _, tok, _ = x.shape
    span = n * tok
    return pl.pallas_call(
        query_kernel,
        out_shape=jax.ShapeDtypeStruct((n, tok, DH), BF16),
        grid_spec=pltpu.PrefetchScalarGridSpec(
            num_scalar_prefetch=1,
            grid=(span // BQ,),
            in_specs=[whole(a.shape) for a in (x, pk, pv)]
            + [
                pl.BlockSpec((BQ, DH), lambda i, s: (i, 0)),
                pl.BlockSpec((8, BQ), lambda i, s: (0, i)),
            ],
            out_specs=pl.BlockSpec((BQ // tok, tok, DH), lambda i, s: (i, 0, 0)),
        ),
        compiler_params=pltpu.CompilerParams(vmem_limit_bytes=62 * MIB),
        cost_estimate=pl.CostEstimate(flops=5 * 10**9, bytes_accessed=6 * 10**6, transcendentals=10**7),
        name="attn_query",
    )(bounds, x, pk, pv, dq_span, stats)


def past_kernel(first, bounds, x_ref, pk_ref, pv_ref, stat_ref, acc_ref, prev_ref, nacc_ref, dk, dv):
    del prev_ref
    offset = bounds[0]
    length = bounds[1]
    kstart = (first + pl.program_id(0)) * BK
    dk[...] = jnp.zeros_like(dk)
    dv[...] = jnp.zeros_like(dv)

    def step(i, carry):
        qstart = pl.multiple_of(i * BQ, BQ)
        q = token_rows(x_ref, 0, qstart, BQ)
        g = live_rows(token_rows(x_ref, 3, qstart, BQ), qstart, length)
        s = mask_past(dot(pk_ref[...], q.T), kstart, offset)
        p = jnp.exp2(s * SCALE_LOG2 - stat_ref[0:1, pl.ds(qstart, BQ)])
        dp = dot(pv_ref[...], g.T)
        ds = (p * (dp - stat_ref[1:2, pl.ds(qstart, BQ)])).astype(BF16)
        dk[...] += dot(ds, q)
        dv[...] += dot(p.astype(BF16), g)
        return carry

    @pl.when(kstart < offset)
    def _():
        lax.fori_loop(0, (length + BQ - 1) // BQ, step, 0)

    even = pl.ds(0, BK, stride=2)
    odd = pl.ds(1, BK, stride=2)
    nacc_ref[even, :] = acc_ref[even, :] + dk[...] * SCALE
    nacc_ref[odd, :] = acc_ref[odd, :] + dv[...]


def past_grads(bounds, x, pk, pv, stats, accum, first, count, prev=None):
    keys = pl.BlockSpec((BK, DH), lambda i, s: (first + i, 0))
    pairs = pl.BlockSpec((2 * BK, DH), lambda i, s: (first + i, 0))
    args = [bounds, x, pk, pv, stats, accum]
    in_specs = [whole(x.shape), keys, keys, whole(stats.shape), pairs]
    body = functools.partial(past_kernel, first)
    aliases = {}
    if prev is None:
        body = lambda *refs: past_kernel(first, *refs[:6], None, *refs[6:])
    else:
        args.append(prev)
        in_specs.append(pl.BlockSpec(memory_space=pl.ANY))
        aliases = {6: 0}
    return pl.pallas_call(
        body,
        out_shape=jax.ShapeDtypeStruct(accum.shape, F32),
        grid_spec=pltpu.PrefetchScalarGridSpec(
            num_scalar_prefetch=1,
            grid=(count,),
            in_specs=in_specs,
            out_specs=pairs,
            scratch_shapes=[pltpu.VMEM((BK, DH), F32), pltpu.VMEM((BK, DH), F32)],
        ),
        input_output_aliases=aliases,
        compiler_params=pltpu.CompilerParams(vmem_limit_bytes=62 * MIB),
        cost_estimate=pl.CostEstimate(
            flops=2 * 10**9 * count, bytes_accessed=4 * 10**6 * count, transcendentals=10**6 * count
        ),
        name=f"attn_past{first}",
    )(*args)


def to_heads(x):
    return lax.all_to_all(x, "seq", split_axis=0, concat_axis=0, tiled=True)


def from_behind(block, axis, distance):
    size = lax.axis_size(axis)
    return lax.ppermute(block, axis, [((i - distance) % size, i) for i in range(size)])


def per_device(span_inputs, out_grad, past_cache, past_accum, offsets, lengths):
    past = past_cache.shape[1]
    bounds = jnp.concatenate([offsets, lengths])
    cache = past_cache.reshape(past, 2, DH)
    pk, pv = cache[:, 0], cache[:, 1]
    x = to_heads(pack(jnp.transpose(span_inputs[0], (1, 0, 2)), out_grad[0]))
    kv, dq_span, stats = span_grads_and_stats(bounds, x, pk, pv)
    kv = to_heads(kv)
    dq = query_grads(bounds, x, pk, pv, dq_span, stats)
    dq, bounds = lax.optimization_barrier((dq, bounds))
    dq = from_behind(dq, "section", -1)
    accum = past_accum.reshape(past * 2, DH)
    new_accum = past_grads(bounds, x, pk, pv, stats, accum, 0, 1)
    kv, dq, new_accum, bounds = lax.optimization_barrier((kv, dq, new_accum, bounds))
    dq = to_heads(dq)
    kv = from_behind(kv, "section", -1)
    new_accum = past_grads(bounds, x, pk, pv, stats, accum, 1, past // BK - 1, new_accum)
    out = jnp.transpose(unpack(dq, kv), (1, 0, 2))
    return out[None], new_accum.reshape(past_accum.shape)


def solution(mesh):
    in_specs = (
        P("section", "seq", None, None),
        P("section", "seq", None),
        P("section", None, None, "seq", None),
        P("section", None, None, "seq", None),
        P("section"),
        P("section"),
    )
    out_specs = (P("section", "seq", None, None), P("section", None, None, "seq", None))
    return jax.shard_map(
        per_device, mesh=mesh, in_specs=in_specs, out_specs=out_specs, check_vma=False
    )
```

```python
import functools
import math

import jax
import jax.numpy as jnp
from jax import lax
from jax.experimental import pallas as pl
from jax.experimental.pallas import tpu as pltpu
from jax.sharding import PartitionSpec as P


HEADS = 64
DH = 128
NEG = -1e30
SCALE = 1.0 / math.sqrt(DH)
SCALE_LOG2 = SCALE * math.log2(math.e)
F32 = jnp.float32
BF16 = jnp.bfloat16
BQ = 512
BK = 1024
MIB = 2**20


def pack_kernel(chunks, x_hbm, g_hbm, o_hbm, x_ref, g_ref, o_ref, in_sem, out_sem):
    heads = HEADS // chunks
    copies = []
    for c in range(chunks):
        cols = pl.ds(c * heads * DH, heads * DH)
        copies.append((
            pltpu.make_async_copy(x_hbm.at[:, :, cols], x_ref.at[:, :, cols], in_sem.at[0, c]),
            pltpu.make_async_copy(g_hbm.at[:, cols], g_ref.at[:, cols], in_sem.at[1, c]),
        ))
    for pair in copies:
        for copy in pair:
            copy.start()
    stores = []
    for c in range(chunks):
        for copy in copies[c]:
            copy.wait()
        for h in range(c * heads, (c + 1) * heads):
            cols = slice(h * DH, (h + 1) * DH)
            for p in range(3):
                o_ref[h, p] = x_ref[p, :, cols]
            o_ref[h, 3] = g_ref[:, cols]
        rows = pl.ds(c * heads, heads)
        stores.append(pltpu.make_async_copy(o_ref.at[rows], o_hbm.at[rows], out_sem.at[c]))
        stores[-1].start()
    for store in stores:
        store.wait()


def pack(x, g, chunks=8):
    shape = (HEADS, 4, x.shape[1], DH)
    hbm = pl.BlockSpec(memory_space=pl.ANY)
    return pl.pallas_call(
        functools.partial(pack_kernel, chunks),
        out_shape=jax.ShapeDtypeStruct(shape, BF16),
        in_specs=[hbm, hbm],
        out_specs=hbm,
        scratch_shapes=[
            pltpu.VMEM(x.shape, BF16),
            pltpu.VMEM(g.shape, BF16),
            pltpu.VMEM(shape, BF16),
            pltpu.SemaphoreType.DMA((2, chunks)),
            pltpu.SemaphoreType.DMA((chunks,)),
        ],
        compiler_params=pltpu.CompilerParams(vmem_limit_bytes=62 * MIB),
        name="pack",
    )(x, g)


def unpack_kernel(q_ref, kv_ref, o_ref):
    for h in range(q_ref.shape[0]):
        cols = slice(h * DH, (h + 1) * DH)
        o_ref[0, :, cols] = q_ref[h]
        o_ref[1, :, cols] = kv_ref[h, 0]
        o_ref[2, :, cols] = kv_ref[h, 1]


def unpack(q, kv, heads_per_step=16):
    rows = q.shape[1]
    return pl.pallas_call(
        unpack_kernel,
        out_shape=jax.ShapeDtypeStruct((3, rows, HEADS * DH), BF16),
        grid=(HEADS // heads_per_step,),
        in_specs=[
            pl.BlockSpec((heads_per_step, rows, DH), lambda i: (i, 0, 0)),
            pl.BlockSpec((heads_per_step, 2, rows, DH), lambda i: (i, 0, 0, 0)),
        ],
        out_specs=pl.BlockSpec((3, rows, heads_per_step * DH), lambda i: (0, 0, i)),
        compiler_params=pltpu.CompilerParams(vmem_limit_bytes=16 * MIB),
        name="unpack",
    )(q, kv)


def whole(shape):
    return pl.BlockSpec(shape, lambda i, s: (0,) * len(shape), pipeline_mode=pl.Buffered(1))


def dot(a, b):
    return jnp.dot(a, b, preferred_element_type=F32)


def dot_rows(a, b):
    return lax.dot_general(a, b, (((0,), (0,)), ((), ())), preferred_element_type=F32)


def token_rows(x_ref, plane, start, count):
    tok = x_ref.shape[2]
    return x_ref[pl.ds(start // tok, count // tok), plane].reshape(count, DH)


def live_rows(g, start, length):
    row = start + lax.broadcasted_iota(jnp.int32, g.shape, 0)
    return jnp.where(row < length, g, jnp.zeros_like(g))


def fold(x, op):
    return op(x.reshape(x.shape[0] // 8, 8, x.shape[1]), axis=0)


def mask_past(s, r0, offset):
    key = r0 + lax.broadcasted_iota(jnp.int32, s.shape, 0)
    return jnp.where(key < offset, s, NEG)


def past_copies(pk_hbm, pv_hbm, pk_ref, pv_ref, sems, b):
    rows = pl.ds(pl.multiple_of(b * BK, BK), BK)
    return (
        pltpu.make_async_copy(pk_hbm.at[rows], pk_ref.at[rows], sems.at[0, b]),
        pltpu.make_async_copy(pv_hbm.at[rows], pv_ref.at[rows], sems.at[1, b]),
    )


def each(count, action):
    def body(b, carry):
        action(b)
        return carry

    lax.fori_loop(0, count, body, 0)


def span_kernel(
    bounds, x_hbm, pk_hbm, pv_hbm, okv_ref, dq_ref, stat_ref,
    x_ref, pk_ref, pv_ref, s_sc, dp_sc, dka, dva, x_sem, past_sem,
):
    n, _, tok, _ = x_ref.shape
    i = pl.program_id(0)
    offset = bounds[0]
    length = bounds[1]
    qstart = i * BQ
    n_past = (offset + BK - 1) // BK

    def x_copy(c):
        rows = pl.ds(c * (BQ // tok), BQ // tok)
        return pltpu.make_async_copy(x_hbm.at[rows], x_ref.at[rows], x_sem.at[c])

    def start_past(b):
        for copy in past_copies(pk_hbm, pv_hbm, pk_ref, pv_ref, past_sem, b):
            copy.start()

    def wait_past(b):
        @pl.when(i == 0)
        def _():
            for copy in past_copies(pk_hbm, pv_hbm, pk_ref, pv_ref, past_sem, b):
                copy.wait()

    @pl.when(i == 0)
    def _():
        x_copy(0).start()
        each(n_past, start_past)
        for c in range(1, n * tok // BQ):
            x_copy(c).start()

    @pl.when(i == 0)
    def _():
        dka[...] = jnp.zeros_like(dka)
        dva[...] = jnp.zeros_like(dva)

    x_copy(i).wait()

    @pl.when(qstart >= length)
    def _():
        dq_ref[...] = jnp.zeros_like(dq_ref)
        stat_ref[...] = jnp.zeros_like(stat_ref)
        each(n_past, wait_past)

    @pl.when(qstart < length)
    def _():
        q = token_rows(x_ref, 0, qstart, BQ)
        g = live_rows(token_rows(x_ref, 3, qstart, BQ), qstart, length)
        q_t = q.T
        g_t = g.T
        half = BQ // 2
        lo = pl.ds(pl.multiple_of(qstart, BQ), half)
        hi = pl.ds(pl.multiple_of(qstart + half, half), half)

        def update(s, dp, carry):
            m, l, d = carry
            m_new = jnp.maximum(m, jnp.max(fold(s, jnp.max), axis=0, keepdims=True))
            keep = jnp.exp2((m - m_new) * SCALE_LOG2)
            e = jnp.exp2(s * SCALE_LOG2 - m_new * SCALE_LOG2)
            return m_new, l * keep + fold(e, jnp.sum), d * keep + fold(e * dp, jnp.sum)

        def past_stats(b, carry, masked):
            wait_past(b)
            r0 = pl.multiple_of(b * BK, BK)
            size = BK // 2
            parts = [pl.ds(r0 + k * size, size) for k in range(2)]
            s = [dot(pk_ref[r, :], q_t) for r in parts]
            dp = [dot(pv_ref[r, :], g_t) for r in parts]
            for k in range(2):
                if masked:
                    s[k] = mask_past(s[k], r0 + k * size, offset)
                carry = update(s[k], dp[k], carry)
            return carry

        def span_stats(b, carry):
            r0 = pl.multiple_of(b * BQ, BQ)
            s = dot(token_rows(x_ref, 1, r0, BQ), q_t)
            dp = dot(token_rows(x_ref, 2, r0, BQ), g_t)
            s_sc[pl.ds(r0, BQ), :] = s
            dp_sc[pl.ds(r0, BQ), :] = dp
            return update(s, dp, carry)

        def diagonal_stats(carry):
            key = lax.broadcasted_iota(jnp.int32, (half, BQ), 0)
            query = lax.broadcasted_iota(jnp.int32, (half, BQ), 1)
            s = dot(token_rows(x_ref, 1, qstart, half), q_t)
            dp = dot(token_rows(x_ref, 2, qstart, half), g_t)
            s_hi = dot(token_rows(x_ref, 1, qstart + half, half), q_t[:, half:])
            dp_hi = dot(token_rows(x_ref, 2, qstart + half, half), g_t[:, half:])
            s = jnp.where((key <= query) & (qstart + key < length), s, NEG)
            s_sc[lo, :] = s
            dp_sc[lo, :] = dp
            carry = update(s, dp, carry)
            key = key[:, :half]
            seen = (key <= query[:, :half]) & (qstart + half + key < length)
            s_hi = jnp.where(seen, s_hi, NEG)
            s_sc[hi, half:] = s_hi
            dp_sc[hi, half:] = dp_hi
            right = update(s_hi, dp_hi, tuple(c[:, half:] for c in carry))
            return tuple(jnp.concatenate([c[:, :half], r], axis=1) for c, r in zip(carry, right))

        zero = jnp.zeros((8, BQ), F32)
        carry = (jnp.full((1, BQ), NEG, F32), zero, zero)
        carry = lax.fori_loop(0, i, span_stats, carry)
        carry = diagonal_stats(carry)
        full = offset // BK
        carry = lax.fori_loop(0, full, functools.partial(past_stats, masked=False), carry)
        m, l, d = lax.fori_loop(
            full, n_past, functools.partial(past_stats, masked=True), carry
        )
        l = jnp.sum(l, axis=0, keepdims=True)
        delta = jnp.sum(d, axis=0, keepdims=True) / l
        lse = m * SCALE_LOG2 + jnp.log2(l)
        stat_ref[...] = jnp.concatenate([lse, delta, jnp.zeros((6, BQ), F32)], axis=0)

        def p_and_ds(rows, cols):
            p = jnp.exp2(s_sc[rows, cols] * SCALE_LOG2 - lse[:, cols])
            return p.astype(BF16), (p * (dp_sc[rows, cols] - delta[:, cols])).astype(BF16)

        def span_grads(b, dq):
            rows = pl.ds(pl.multiple_of(b * BQ, BQ), BQ)
            p, ds = p_and_ds(rows, slice(0, BQ))
            dva[rows, :] += dot(p, g)
            dka[rows, :] += dot(ds, q)
            return dq + dot_rows(ds, token_rows(x_ref, 1, b * BQ, BQ))

        dq = lax.fori_loop(0, i, span_grads, jnp.zeros((BQ, DH), F32))
        p, ds = p_and_ds(lo, slice(0, BQ))
        p_hi, ds_hi = p_and_ds(hi, slice(half, BQ))
        dva[lo, :] += dot(p, g)
        dka[lo, :] += dot(ds, q)
        dva[hi, :] += dot(p_hi, g[half:])
        dka[hi, :] += dot(ds_hi, q[half:])
        dq = dq + dot_rows(ds, token_rows(x_ref, 1, qstart, half))
        dq_ref[:half] = dq[:half]
        dq_ref[half:] = dq[half:] + dot_rows(ds_hi, token_rows(x_ref, 1, qstart + half, half))

    @pl.when(i == pl.num_programs(0) - 1)
    def _():
        okv_ref[:, 0] = (dka[...] * SCALE).astype(BF16).reshape(n, tok, DH)
        okv_ref[:, 1] = dva[...].astype(BF16).reshape(n, tok, DH)


def span_grads_and_stats(bounds, x, pk, pv):
    n, _, tok, _ = x.shape
    span = n * tok
    return pl.pallas_call(
        span_kernel,
        out_shape=(
            jax.ShapeDtypeStruct((n, 2, tok, DH), BF16),
            jax.ShapeDtypeStruct((span, DH), F32),
            jax.ShapeDtypeStruct((8, span), F32),
        ),
        grid_spec=pltpu.PrefetchScalarGridSpec(
            num_scalar_prefetch=1,
            grid=(span // BQ,),
            in_specs=[pl.BlockSpec(memory_space=pl.ANY)] * 3,
            out_specs=(
                whole((n, 2, tok, DH)),
                pl.BlockSpec((BQ, DH), lambda i, s: (i, 0)),
                pl.BlockSpec((8, BQ), lambda i, s: (0, i)),
            ),
            scratch_shapes=[
                pltpu.VMEM(x.shape, BF16),
                pltpu.VMEM(pk.shape, BF16),
                pltpu.VMEM(pv.shape, BF16),
                pltpu.VMEM((span, BQ), F32),
                pltpu.VMEM((span, BQ), F32),
                pltpu.VMEM((span, DH), F32),
                pltpu.VMEM((span, DH), F32),
                pltpu.SemaphoreType.DMA((span // BQ,)),
                pltpu.SemaphoreType.DMA((2, pk.shape[0] // BK)),
            ],
        ),
        compiler_params=pltpu.CompilerParams(vmem_limit_bytes=62 * MIB),
        cost_estimate=pl.CostEstimate(flops=7 * 10**9, bytes_accessed=6 * 10**6, transcendentals=10**7),
        name="attn_span",
    )(bounds, x, pk, pv)


def query_kernel(
    first, bounds, q_ref, g_ref, pk_hbm, pv_hbm, dqs_ref, stat_ref, o_ref, pk_ref, pv_ref, past_sem
):
    tok = q_ref.shape[2]
    i = pl.program_id(0)
    offset = bounds[0]
    length = bounds[1]
    qstart = (first + i) * BQ
    n_past = (offset + BK - 1) // BK

    def start_past(b):
        for copy in past_copies(pk_hbm, pv_hbm, pk_ref, pv_ref, past_sem, b):
            copy.start()

    def wait_past(b):
        @pl.when(i == 0)
        def _():
            for copy in past_copies(pk_hbm, pv_hbm, pk_ref, pv_ref, past_sem, b):
                copy.wait()

    @pl.when(i == 0)
    def _():
        each(n_past, start_past)

    @pl.when(qstart >= length)
    def _():
        o_ref[...] = jnp.zeros_like(o_ref)
        each(n_past, wait_past)

    @pl.when(qstart < length)
    def _():
        q_t = q_ref[:, 0].reshape(BQ, DH).T
        g_t = live_rows(g_ref[:, 0].reshape(BQ, DH), qstart, length).T
        lse = stat_ref[0:1]
        delta = stat_ref[1:2]

        def step(b, dq):
            wait_past(b)
            r0 = pl.multiple_of(b * BK, BK)
            keys = pk_ref[pl.ds(r0, BK), :]
            p = jnp.exp2(mask_past(dot(keys, q_t), r0, offset) * SCALE_LOG2 - lse)
            dp = dot(pv_ref[pl.ds(r0, BK), :], g_t)
            ds = (p * (dp - delta)).astype(BF16)
            return dq + dot_rows(ds, keys)

        dq = lax.fori_loop(0, n_past, step, dqs_ref[...])
        o_ref[...] = (dq * SCALE).astype(BF16).reshape(BQ // tok, tok, DH)


def query_grads(bounds, x, pk, pv, dq_span, stats, first, count):
    _, _, tok, _ = x.shape
    group = BQ // tok
    hbm = pl.BlockSpec(memory_space=pl.ANY)
    return pl.pallas_call(
        functools.partial(query_kernel, first),
        out_shape=jax.ShapeDtypeStruct((count * group, tok, DH), BF16),
        grid_spec=pltpu.PrefetchScalarGridSpec(
            num_scalar_prefetch=1,
            grid=(count,),
            in_specs=[
                pl.BlockSpec((group, 1, tok, DH), lambda i, s: (first + i, 0, 0, 0)),
                pl.BlockSpec((group, 1, tok, DH), lambda i, s: (first + i, 3, 0, 0)),
                hbm,
                hbm,
                pl.BlockSpec((BQ, DH), lambda i, s: (first + i, 0)),
                pl.BlockSpec((8, BQ), lambda i, s: (0, first + i)),
            ],
            out_specs=pl.BlockSpec((group, tok, DH), lambda i, s: (i, 0, 0)),
            scratch_shapes=[
                pltpu.VMEM(pk.shape, BF16),
                pltpu.VMEM(pv.shape, BF16),
                pltpu.SemaphoreType.DMA((2, pk.shape[0] // BK)),
            ],
        ),
        compiler_params=pltpu.CompilerParams(vmem_limit_bytes=62 * MIB),
        cost_estimate=pl.CostEstimate(
            flops=10**9 * count, bytes_accessed=10**6 * count, transcendentals=2 * 10**6 * count
        ),
    )(bounds, x, x, pk, pv, dq_span, stats)


def past_kernel(first, bounds, x_ref, pk_ref, pv_ref, stat_ref, acc_ref, prev_ref, nacc_ref, dk, dv):
    del prev_ref
    offset = bounds[0]
    length = bounds[1]
    kstart = (first + pl.program_id(0)) * BK
    dk[...] = jnp.zeros_like(dk)
    dv[...] = jnp.zeros_like(dv)

    def step(i, carry):
        qstart = pl.multiple_of(i * BQ, BQ)
        q = token_rows(x_ref, 0, qstart, BQ)
        g = live_rows(token_rows(x_ref, 3, qstart, BQ), qstart, length)
        s = mask_past(dot(pk_ref[...], q.T), kstart, offset)
        p = jnp.exp2(s * SCALE_LOG2 - stat_ref[0:1, pl.ds(qstart, BQ)])
        dp = dot(pv_ref[...], g.T)
        ds = (p * (dp - stat_ref[1:2, pl.ds(qstart, BQ)])).astype(BF16)
        dk[...] += dot(ds, q)
        dv[...] += dot(p.astype(BF16), g)
        return carry

    @pl.when(kstart < offset)
    def _():
        lax.fori_loop(0, (length + BQ - 1) // BQ, step, 0)

    even = pl.ds(0, BK, stride=2)
    odd = pl.ds(1, BK, stride=2)
    nacc_ref[even, :] = acc_ref[even, :] + dk[...] * SCALE
    nacc_ref[odd, :] = acc_ref[odd, :] + dv[...]


def past_grads(bounds, x, pk, pv, stats, accum, first, count, prev=None):
    keys = pl.BlockSpec((BK, DH), lambda i, s: (first + i, 0))
    pairs = pl.BlockSpec((2 * BK, DH), lambda i, s: (first + i, 0))
    args = [bounds, x, pk, pv, stats, accum]
    in_specs = [whole(x.shape), keys, keys, whole(stats.shape), pairs]
    body = functools.partial(past_kernel, first)
    aliases = {}
    if prev is None:
        body = lambda *refs: past_kernel(first, *refs[:6], None, *refs[6:])
    else:
        args.append(prev)
        in_specs.append(pl.BlockSpec(memory_space=pl.ANY))
        aliases = {6: 0}
    return pl.pallas_call(
        body,
        out_shape=jax.ShapeDtypeStruct(accum.shape, F32),
        grid_spec=pltpu.PrefetchScalarGridSpec(
            num_scalar_prefetch=1,
            grid=(count,),
            in_specs=in_specs,
            out_specs=pairs,
            scratch_shapes=[pltpu.VMEM((BK, DH), F32), pltpu.VMEM((BK, DH), F32)],
        ),
        input_output_aliases=aliases,
        compiler_params=pltpu.CompilerParams(vmem_limit_bytes=62 * MIB),
        cost_estimate=pl.CostEstimate(
            flops=2 * 10**9 * count, bytes_accessed=4 * 10**6 * count, transcendentals=10**6 * count
        ),
    )(*args)


def to_heads(x):
    return lax.all_to_all(x, "seq", split_axis=0, concat_axis=0, tiled=True)


def from_behind(block, axis, distance):
    size = lax.axis_size(axis)
    return lax.ppermute(block, axis, [((i - distance) % size, i) for i in range(size)])


def per_device(span_inputs, out_grad, past_cache, past_accum, offsets, lengths):
    past = past_cache.shape[1]
    bounds = jnp.concatenate([offsets, lengths])
    cache = past_cache.reshape(past, 2, DH)
    pk, pv = cache[:, 0], cache[:, 1]
    x = to_heads(pack(jnp.transpose(span_inputs[0], (1, 0, 2)), out_grad[0]))
    kv, dq_span, stats = span_grads_and_stats(bounds, x, pk, pv)
    kv = to_heads(kv)
    half = x.shape[0] * x.shape[2] // BQ // 2
    low = query_grads(bounds, x, pk, pv, dq_span, stats, 0, half)
    low, bounds = lax.optimization_barrier((low, bounds))
    low = from_behind(low, "section", -1)
    high = query_grads(bounds, x, pk, pv, dq_span, stats, half, half)
    high, bounds = lax.optimization_barrier((high, bounds))
    high = from_behind(high, "section", -1)
    accum = past_accum.reshape(past * 2, DH)
    new_accum = past_grads(bounds, x, pk, pv, stats, accum, 0, 1)
    kv, dq, new_accum, bounds = lax.optimization_barrier(
        (kv, jnp.concatenate([low, high]), new_accum, bounds)
    )
    dq = to_heads(dq)
    kv = from_behind(kv, "section", -1)
    new_accum = past_grads(bounds, x, pk, pv, stats, accum, 1, past // BK - 1, new_accum)
    out = jnp.transpose(unpack(dq, kv), (1, 0, 2))
    return out[None], new_accum.reshape(past_accum.shape)


def solution(mesh):
    in_specs = (
        P("section", "seq", None, None),
        P("section", "seq", None),
        P("section", None, None, "seq", None),
        P("section", None, None, "seq", None),
        P("section"),
        P("section"),
    )
    out_specs = (P("section", "seq", None, None), P("section", None, None, "seq", None))
    return jax.shard_map(
        per_device, mesh=mesh, in_specs=in_specs, out_specs=out_specs, check_vma=False
    )
```

```python
import functools
import math

import jax
import jax.numpy as jnp
from jax import lax
from jax.experimental import pallas as pl
from jax.experimental.pallas import tpu as pltpu
from jax.sharding import PartitionSpec as P


HEADS = 64
DH = 128
NEG = -1e30
SCALE = 1.0 / math.sqrt(DH)
SCALE_LOG2 = SCALE * math.log2(math.e)
F32 = jnp.float32
BF16 = jnp.bfloat16
BQ = 512
BK = 1024
MIB = 2**20


def pack_kernel(chunks, x_hbm, g_hbm, o_hbm, x_ref, g_ref, o_ref, in_sem, out_sem):
    heads = HEADS // chunks
    copies = []
    for c in range(chunks):
        cols = pl.ds(c * heads * DH, heads * DH)
        copies.append((
            pltpu.make_async_copy(x_hbm.at[:, :, cols], x_ref.at[:, :, cols], in_sem.at[0, c]),
            pltpu.make_async_copy(g_hbm.at[:, cols], g_ref.at[:, cols], in_sem.at[1, c]),
        ))
    for pair in copies:
        for copy in pair:
            copy.start()
    stores = []
    for c in range(chunks):
        for copy in copies[c]:
            copy.wait()
        for h in range(c * heads, (c + 1) * heads):
            cols = slice(h * DH, (h + 1) * DH)
            for p in range(3):
                o_ref[h, p] = x_ref[p, :, cols]
            o_ref[h, 3] = g_ref[:, cols]
        rows = pl.ds(c * heads, heads)
        stores.append(pltpu.make_async_copy(o_ref.at[rows], o_hbm.at[rows], out_sem.at[c]))
        stores[-1].start()
    for store in stores:
        store.wait()


def pack(x, g, chunks=8):
    shape = (HEADS, 4, x.shape[1], DH)
    hbm = pl.BlockSpec(memory_space=pl.ANY)
    return pl.pallas_call(
        functools.partial(pack_kernel, chunks),
        out_shape=jax.ShapeDtypeStruct(shape, BF16),
        in_specs=[hbm, hbm],
        out_specs=hbm,
        scratch_shapes=[
            pltpu.VMEM(x.shape, BF16),
            pltpu.VMEM(g.shape, BF16),
            pltpu.VMEM(shape, BF16),
            pltpu.SemaphoreType.DMA((2, chunks)),
            pltpu.SemaphoreType.DMA((chunks,)),
        ],
        compiler_params=pltpu.CompilerParams(vmem_limit_bytes=62 * MIB),
        name="pack",
    )(x, g)


def unpack_kernel(chunks, q_ref, kv_ref, o_hbm, o_ref, sem):
    heads = HEADS // chunks
    stores = []
    for c in range(chunks):
        for h in range(c * heads, (c + 1) * heads):
            cols = slice(h * DH, (h + 1) * DH)
            o_ref[0, :, cols] = q_ref[h]
            o_ref[1, :, cols] = kv_ref[h, 0]
            o_ref[2, :, cols] = kv_ref[h, 1]
        cols = pl.ds(c * heads * DH, heads * DH)
        stores.append(pltpu.make_async_copy(o_ref.at[:, :, cols], o_hbm.at[:, :, cols], sem.at[c]))
        stores[-1].start()
    for store in stores:
        store.wait()


def unpack(q, kv, chunks=8):
    shape = (3, q.shape[1], HEADS * DH)
    vmem = pl.BlockSpec(memory_space=pltpu.VMEM)
    return pl.pallas_call(
        functools.partial(unpack_kernel, chunks),
        out_shape=jax.ShapeDtypeStruct(shape, BF16),
        in_specs=[vmem, vmem],
        out_specs=pl.BlockSpec(memory_space=pl.ANY),
        scratch_shapes=[pltpu.VMEM(shape, BF16), pltpu.SemaphoreType.DMA((chunks,))],
        compiler_params=pltpu.CompilerParams(vmem_limit_bytes=16 * MIB),
        name="unpack",
    )(q, kv)


def whole(shape):
    return pl.BlockSpec(shape, lambda i: (0,) * len(shape), pipeline_mode=pl.Buffered(1))


def scalars():
    return pl.BlockSpec(memory_space=pltpu.SMEM)


def dot(a, b):
    return jnp.dot(a, b, preferred_element_type=F32)


def dot_rows(a, b):
    return lax.dot_general(a, b, (((0,), (0,)), ((), ())), preferred_element_type=F32)


def token_rows(x_ref, plane, start, count):
    tok = x_ref.shape[2]
    return x_ref[pl.ds(start // tok, count // tok), plane].reshape(count, DH)


def live_rows(g, start, length):
    row = start + lax.broadcasted_iota(jnp.int32, g.shape, 0)
    return jnp.where(row < length, g, jnp.zeros_like(g))


def fold(x, op):
    return op(x.reshape(x.shape[0] // 8, 8, x.shape[1]), axis=0)


def mask_past(s, r0, offset):
    key = r0 + lax.broadcasted_iota(jnp.int32, s.shape, 0)
    return jnp.where(key < offset, s, NEG)


def past_copies(pk_hbm, pv_hbm, pk_ref, pv_ref, sems, b):
    rows = pl.ds(pl.multiple_of(b * BK, BK), BK)
    return (
        pltpu.make_async_copy(pk_hbm.at[rows], pk_ref.at[rows], sems.at[0, b]),
        pltpu.make_async_copy(pv_hbm.at[rows], pv_ref.at[rows], sems.at[1, b]),
    )


def each(count, action):
    def body(b, carry):
        action(b)
        return carry

    lax.fori_loop(0, count, body, 0)


def span_kernel(
    bounds, x_hbm, pk_hbm, pv_hbm, okv_ref, dq_ref, stat_ref,
    x_ref, pk_ref, pv_ref, s_sc, dp_sc, dka, dva, x_sem, past_sem,
):
    n, _, tok, _ = x_ref.shape
    i = pl.program_id(0)
    offset = bounds[0]
    length = bounds[1]
    qstart = i * BQ
    n_past = (offset + BK - 1) // BK

    def x_copy(c):
        rows = pl.ds(c * (BQ // tok), BQ // tok)
        return pltpu.make_async_copy(x_hbm.at[rows], x_ref.at[rows], x_sem.at[c])

    def start_past(b):
        for copy in past_copies(pk_hbm, pv_hbm, pk_ref, pv_ref, past_sem, b):
            copy.start()

    def wait_past(b):
        @pl.when(i == 0)
        def _():
            for copy in past_copies(pk_hbm, pv_hbm, pk_ref, pv_ref, past_sem, b):
                copy.wait()

    @pl.when(i == 0)
    def _():
        x_copy(0).start()
        each(n_past, start_past)
        for c in range(1, n * tok // BQ):
            x_copy(c).start()

    @pl.when(i == 0)
    def _():
        dka[...] = jnp.zeros_like(dka)
        dva[...] = jnp.zeros_like(dva)

    x_copy(i).wait()

    @pl.when(qstart >= length)
    def _():
        dq_ref[...] = jnp.zeros_like(dq_ref)
        stat_ref[...] = jnp.zeros_like(stat_ref)
        each(n_past, wait_past)

    @pl.when(qstart < length)
    def _():
        q = token_rows(x_ref, 0, qstart, BQ)
        g = live_rows(token_rows(x_ref, 3, qstart, BQ), qstart, length)
        q_t = q.T
        g_t = g.T
        half = BQ // 2
        lo = pl.ds(pl.multiple_of(qstart, BQ), half)
        hi = pl.ds(pl.multiple_of(qstart + half, half), half)

        def update(s, dp, carry):
            m, l, d = carry
            m_new = jnp.maximum(m, jnp.max(fold(s, jnp.max), axis=0, keepdims=True))
            keep = jnp.exp2((m - m_new) * SCALE_LOG2)
            e = jnp.exp2(s * SCALE_LOG2 - m_new * SCALE_LOG2)
            return m_new, l * keep + fold(e, jnp.sum), d * keep + fold(e * dp, jnp.sum)

        def past_stats(b, carry, masked):
            wait_past(b)
            r0 = pl.multiple_of(b * BK, BK)
            size = BK // 2
            parts = [pl.ds(r0 + k * size, size) for k in range(2)]
            s = [dot(pk_ref[r, :], q_t) for r in parts]
            dp = [dot(pv_ref[r, :], g_t) for r in parts]
            for k in range(2):
                if masked:
                    s[k] = mask_past(s[k], r0 + k * size, offset)
                carry = update(s[k], dp[k], carry)
            return carry

        def span_stats(b, carry):
            r0 = pl.multiple_of(b * BQ, BQ)
            s = dot(token_rows(x_ref, 1, r0, BQ), q_t)
            dp = dot(token_rows(x_ref, 2, r0, BQ), g_t)
            s_sc[pl.ds(r0, BQ), :] = s
            dp_sc[pl.ds(r0, BQ), :] = dp
            return update(s, dp, carry)

        def diagonal_stats(carry):
            key = lax.broadcasted_iota(jnp.int32, (half, BQ), 0)
            query = lax.broadcasted_iota(jnp.int32, (half, BQ), 1)
            s = dot(token_rows(x_ref, 1, qstart, half), q_t)
            dp = dot(token_rows(x_ref, 2, qstart, half), g_t)
            s_hi = dot(token_rows(x_ref, 1, qstart + half, half), q_t[:, half:])
            dp_hi = dot(token_rows(x_ref, 2, qstart + half, half), g_t[:, half:])
            s = jnp.where((key <= query) & (qstart + key < length), s, NEG)
            s_sc[lo, :] = s
            dp_sc[lo, :] = dp
            carry = update(s, dp, carry)
            key = key[:, :half]
            seen = (key <= query[:, :half]) & (qstart + half + key < length)
            s_hi = jnp.where(seen, s_hi, NEG)
            s_sc[hi, half:] = s_hi
            dp_sc[hi, half:] = dp_hi
            right = update(s_hi, dp_hi, tuple(c[:, half:] for c in carry))
            return tuple(jnp.concatenate([c[:, :half], r], axis=1) for c, r in zip(carry, right))

        zero = jnp.zeros((8, BQ), F32)
        carry = (jnp.full((1, BQ), NEG, F32), zero, zero)
        carry = lax.fori_loop(0, i, span_stats, carry)
        carry = diagonal_stats(carry)
        full = offset // BK
        carry = lax.fori_loop(0, full, functools.partial(past_stats, masked=False), carry)
        m, l, d = lax.fori_loop(
            full, n_past, functools.partial(past_stats, masked=True), carry
        )
        l = jnp.sum(l, axis=0, keepdims=True)
        delta = jnp.sum(d, axis=0, keepdims=True) / l
        lse = m * SCALE_LOG2 + jnp.log2(l)
        stat_ref[...] = jnp.concatenate([lse, delta, jnp.zeros((6, BQ), F32)], axis=0)

        def p_and_ds(rows, cols):
            p = jnp.exp2(s_sc[rows, cols] * SCALE_LOG2 - lse[:, cols])
            return p.astype(BF16), (p * (dp_sc[rows, cols] - delta[:, cols])).astype(BF16)

        def span_grads(b, dq):
            rows = pl.ds(pl.multiple_of(b * BQ, BQ), BQ)
            p, ds = p_and_ds(rows, slice(0, BQ))
            dva[rows, :] += dot(p, g)
            dka[rows, :] += dot(ds, q)
            return dq + dot_rows(ds, token_rows(x_ref, 1, b * BQ, BQ))

        dq = lax.fori_loop(0, i, span_grads, jnp.zeros((BQ, DH), F32))
        p, ds = p_and_ds(lo, slice(0, BQ))
        p_hi, ds_hi = p_and_ds(hi, slice(half, BQ))
        dva[lo, :] += dot(p, g)
        dka[lo, :] += dot(ds, q)
        dva[hi, :] += dot(p_hi, g[half:])
        dka[hi, :] += dot(ds_hi, q[half:])
        dq = dq + dot_rows(ds, token_rows(x_ref, 1, qstart, half))
        dq_ref[:half] = dq[:half]
        dq_ref[half:] = dq[half:] + dot_rows(ds_hi, token_rows(x_ref, 1, qstart + half, half))

    @pl.when(i == pl.num_programs(0) - 1)
    def _():
        okv_ref[:, 0] = (dka[...] * SCALE).astype(BF16).reshape(n, tok, DH)
        okv_ref[:, 1] = dva[...].astype(BF16).reshape(n, tok, DH)


def span_grads_and_stats(bounds, x, pk, pv):
    n, _, tok, _ = x.shape
    span = n * tok
    return pl.pallas_call(
        span_kernel,
        out_shape=(
            jax.ShapeDtypeStruct((n, 2, tok, DH), BF16),
            jax.ShapeDtypeStruct((span, DH), F32),
            jax.ShapeDtypeStruct((8, span), F32),
        ),
        grid_spec=pl.GridSpec(
            grid=(span // BQ,),
            in_specs=[scalars()] + [pl.BlockSpec(memory_space=pl.ANY)] * 3,
            out_specs=(
                whole((n, 2, tok, DH)),
                pl.BlockSpec((BQ, DH), lambda i: (i, 0)),
                pl.BlockSpec((8, BQ), lambda i: (0, i)),
            ),
            scratch_shapes=[
                pltpu.VMEM(x.shape, BF16),
                pltpu.VMEM(pk.shape, BF16),
                pltpu.VMEM(pv.shape, BF16),
                pltpu.VMEM((span, BQ), F32),
                pltpu.VMEM((span, BQ), F32),
                pltpu.VMEM((span, DH), F32),
                pltpu.VMEM((span, DH), F32),
                pltpu.SemaphoreType.DMA((span // BQ,)),
                pltpu.SemaphoreType.DMA((2, pk.shape[0] // BK)),
            ],
        ),
        compiler_params=pltpu.CompilerParams(vmem_limit_bytes=62 * MIB),
        cost_estimate=pl.CostEstimate(flops=7 * 10**9, bytes_accessed=6 * 10**6, transcendentals=10**7),
        name="attn_span",
    )(bounds, x, pk, pv)


def query_kernel(
    first, bounds, q_ref, g_ref, pk_hbm, pv_hbm, dqs_ref, stat_ref, o_ref, pk_ref, pv_ref, past_sem
):
    tok = q_ref.shape[2]
    i = pl.program_id(0)
    offset = bounds[0]
    length = bounds[1]
    qstart = (first + i) * BQ
    n_past = (offset + BK - 1) // BK

    def start_past(b):
        for copy in past_copies(pk_hbm, pv_hbm, pk_ref, pv_ref, past_sem, b):
            copy.start()

    def wait_past(b):
        @pl.when(i == 0)
        def _():
            for copy in past_copies(pk_hbm, pv_hbm, pk_ref, pv_ref, past_sem, b):
                copy.wait()

    @pl.when(i == 0)
    def _():
        each(n_past, start_past)

    @pl.when(qstart >= length)
    def _():
        o_ref[...] = jnp.zeros_like(o_ref)
        each(n_past, wait_past)

    @pl.when(qstart < length)
    def _():
        q_t = q_ref[:, 0].reshape(BQ, DH).T
        g_t = live_rows(g_ref[:, 0].reshape(BQ, DH), qstart, length).T
        lse = stat_ref[0:1]
        delta = stat_ref[1:2]

        def step(b, dq):
            wait_past(b)
            r0 = pl.multiple_of(b * BK, BK)
            keys = pk_ref[pl.ds(r0, BK), :]
            p = jnp.exp2(mask_past(dot(keys, q_t), r0, offset) * SCALE_LOG2 - lse)
            dp = dot(pv_ref[pl.ds(r0, BK), :], g_t)
            ds = (p * (dp - delta)).astype(BF16)
            return dq + dot_rows(ds, keys)

        dq = lax.fori_loop(0, n_past, step, dqs_ref[...])
        o_ref[...] = (dq * SCALE).astype(BF16).reshape(BQ // tok, tok, DH)


def query_grads(bounds, x, pk, pv, dq_span, stats, first, count):
    _, _, tok, _ = x.shape
    group = BQ // tok
    hbm = pl.BlockSpec(memory_space=pl.ANY)
    return pl.pallas_call(
        functools.partial(query_kernel, first),
        out_shape=jax.ShapeDtypeStruct((count * group, tok, DH), BF16),
        grid_spec=pl.GridSpec(
            grid=(count,),
            in_specs=[
                scalars(),
                pl.BlockSpec((group, 1, tok, DH), lambda i: (first + i, 0, 0, 0)),
                pl.BlockSpec((group, 1, tok, DH), lambda i: (first + i, 3, 0, 0)),
                hbm,
                hbm,
                pl.BlockSpec((BQ, DH), lambda i: (first + i, 0)),
                pl.BlockSpec((8, BQ), lambda i: (0, first + i)),
            ],
            out_specs=pl.BlockSpec((group, tok, DH), lambda i: (i, 0, 0)),
            scratch_shapes=[
                pltpu.VMEM(pk.shape, BF16),
                pltpu.VMEM(pv.shape, BF16),
                pltpu.SemaphoreType.DMA((2, pk.shape[0] // BK)),
            ],
        ),
        compiler_params=pltpu.CompilerParams(vmem_limit_bytes=62 * MIB),
        cost_estimate=pl.CostEstimate(
            flops=10**9 * count, bytes_accessed=10**6 * count, transcendentals=2 * 10**6 * count
        ),
    )(bounds, x, x, pk, pv, dq_span, stats)


def past_kernel(first, bounds, x_ref, pk_ref, pv_ref, stat_ref, acc_ref, prev_ref, nacc_ref, dk, dv):
    del prev_ref
    offset = bounds[0]
    length = bounds[1]
    kstart = (first + pl.program_id(0)) * BK
    dk[...] = jnp.zeros_like(dk)
    dv[...] = jnp.zeros_like(dv)

    def step(i, carry):
        qstart = pl.multiple_of(i * BQ, BQ)
        q = token_rows(x_ref, 0, qstart, BQ)
        g = live_rows(token_rows(x_ref, 3, qstart, BQ), qstart, length)
        s = mask_past(dot(pk_ref[...], q.T), kstart, offset)
        p = jnp.exp2(s * SCALE_LOG2 - stat_ref[0:1, pl.ds(qstart, BQ)])
        dp = dot(pv_ref[...], g.T)
        ds = (p * (dp - stat_ref[1:2, pl.ds(qstart, BQ)])).astype(BF16)
        dk[...] += dot(ds, q)
        dv[...] += dot(p.astype(BF16), g)
        return carry

    @pl.when(kstart < offset)
    def _():
        lax.fori_loop(0, (length + BQ - 1) // BQ, step, 0)

    even = pl.ds(0, BK, stride=2)
    odd = pl.ds(1, BK, stride=2)
    nacc_ref[even, :] = acc_ref[even, :] + dk[...] * SCALE
    nacc_ref[odd, :] = acc_ref[odd, :] + dv[...]


def past_grads(bounds, x, pk, pv, stats, accum, first, count, prev=None):
    keys = pl.BlockSpec((BK, DH), lambda i: (first + i, 0))
    pairs = pl.BlockSpec((2 * BK, DH), lambda i: (first + i, 0))
    args = [bounds, x, pk, pv, stats, accum]
    in_specs = [scalars(), whole(x.shape), keys, keys, whole(stats.shape), pairs]
    body = functools.partial(past_kernel, first)
    aliases = {}
    if prev is None:
        body = lambda *refs: past_kernel(first, *refs[:6], None, *refs[6:])
    else:
        args.append(prev)
        in_specs.append(pl.BlockSpec(memory_space=pl.ANY))
        aliases = {6: 0}
    return pl.pallas_call(
        body,
        out_shape=jax.ShapeDtypeStruct(accum.shape, F32),
        grid_spec=pl.GridSpec(
            grid=(count,),
            in_specs=in_specs,
            out_specs=pairs,
            scratch_shapes=[pltpu.VMEM((BK, DH), F32), pltpu.VMEM((BK, DH), F32)],
        ),
        input_output_aliases=aliases,
        compiler_params=pltpu.CompilerParams(vmem_limit_bytes=62 * MIB),
        cost_estimate=pl.CostEstimate(
            flops=2 * 10**9 * count, bytes_accessed=4 * 10**6 * count, transcendentals=10**6 * count
        ),
    )(*args)


def to_heads(x):
    return lax.all_to_all(x, "seq", split_axis=0, concat_axis=0, tiled=True)


def from_behind(block, axis, distance):
    size = lax.axis_size(axis)
    return lax.ppermute(block, axis, [((i - distance) % size, i) for i in range(size)])


def per_device(span_inputs, out_grad, past_cache, past_accum, offsets, lengths):
    past = past_cache.shape[1]
    bounds = jnp.concatenate([offsets, lengths])
    cache = past_cache.reshape(past, 2, DH)
    pk, pv = cache[:, 0], cache[:, 1]
    x = to_heads(pack(jnp.transpose(span_inputs[0], (1, 0, 2)), out_grad[0]))
    kv, dq_span, stats = span_grads_and_stats(bounds, x, pk, pv)
    kv = to_heads(kv)
    half = x.shape[0] * x.shape[2] // BQ // 2
    low = query_grads(bounds, x, pk, pv, dq_span, stats, 0, half)
    low, bounds = lax.optimization_barrier((low, bounds))
    low = from_behind(low, "section", -1)
    high = query_grads(bounds, x, pk, pv, dq_span, stats, half, half)
    high, bounds = lax.optimization_barrier((high, bounds))
    high = from_behind(high, "section", -1)
    accum = past_accum.reshape(past * 2, DH)
    new_accum = past_grads(bounds, x, pk, pv, stats, accum, 0, 1)
    kv, dq, new_accum, bounds = lax.optimization_barrier(
        (kv, jnp.concatenate([low, high]), new_accum, bounds)
    )
    dq = to_heads(dq)
    kv = from_behind(kv, "section", -1)
    new_accum = past_grads(bounds, x, pk, pv, stats, accum, 1, past // BK - 1, new_accum)
    out = jnp.transpose(unpack(dq, kv), (1, 0, 2))
    return out[None], new_accum.reshape(past_accum.shape)


def solution(mesh):
    in_specs = (
        P("section", "seq", None, None),
        P("section", "seq", None),
        P("section", None, None, "seq", None),
        P("section", None, None, "seq", None),
        P("section"),
        P("section"),
    )
    out_specs = (P("section", "seq", None, None), P("section", None, None, "seq", None))
    return jax.shard_map(
        per_device, mesh=mesh, in_specs=in_specs, out_specs=out_specs, check_vma=False
    )
```

```python
import functools
import math

import jax
import jax.numpy as jnp
from jax import lax
from jax.experimental import pallas as pl
from jax.experimental.pallas import tpu as pltpu
from jax.sharding import PartitionSpec as P


HEADS = 64
DH = 128
NEG = -1e30
SCALE = 1.0 / math.sqrt(DH)
SCALE_LOG2 = SCALE * math.log2(math.e)
F32 = jnp.float32
BF16 = jnp.bfloat16
BQ = 512
BK = 1024
PK = 768
MIB = 2**20


def pack_kernel(chunks, x_hbm, g_hbm, o_hbm, x_ref, g_ref, o_ref, in_sem, out_sem):
    heads = HEADS // chunks
    copies = []
    for c in range(chunks):
        cols = pl.ds(c * heads * DH, heads * DH)
        copies.append((
            pltpu.make_async_copy(x_hbm.at[:, :, cols], x_ref.at[:, :, cols], in_sem.at[0, c]),
            pltpu.make_async_copy(g_hbm.at[:, cols], g_ref.at[:, cols], in_sem.at[1, c]),
        ))
    for pair in copies:
        for copy in pair:
            copy.start()
    stores = []
    for c in range(chunks):
        for copy in copies[c]:
            copy.wait()
        for h in range(c * heads, (c + 1) * heads):
            cols = slice(h * DH, (h + 1) * DH)
            for p in range(3):
                o_ref[h, p] = x_ref[p, :, cols]
            o_ref[h, 3] = g_ref[:, cols]
        rows = pl.ds(c * heads, heads)
        stores.append(pltpu.make_async_copy(o_ref.at[rows], o_hbm.at[rows], out_sem.at[c]))
        stores[-1].start()
    for store in stores:
        store.wait()


def pack(x, g, chunks=8):
    shape = (HEADS, 4, x.shape[1], DH)
    hbm = pl.BlockSpec(memory_space=pl.ANY)
    return pl.pallas_call(
        functools.partial(pack_kernel, chunks),
        out_shape=jax.ShapeDtypeStruct(shape, BF16),
        in_specs=[hbm, hbm],
        out_specs=hbm,
        scratch_shapes=[
            pltpu.VMEM(x.shape, BF16),
            pltpu.VMEM(g.shape, BF16),
            pltpu.VMEM(shape, BF16),
            pltpu.SemaphoreType.DMA((2, chunks)),
            pltpu.SemaphoreType.DMA((chunks,)),
        ],
        compiler_params=pltpu.CompilerParams(vmem_limit_bytes=62 * MIB),
        name="pack",
    )(x, g)


def unpack_kernel(chunks, q_ref, kv_ref, o_hbm, o_ref, sem):
    heads = HEADS // chunks
    stores = []
    for c in range(chunks):
        for h in range(c * heads, (c + 1) * heads):
            cols = slice(h * DH, (h + 1) * DH)
            o_ref[0, :, cols] = q_ref[h]
            o_ref[1, :, cols] = kv_ref[h, 0]
            o_ref[2, :, cols] = kv_ref[h, 1]
        cols = pl.ds(c * heads * DH, heads * DH)
        stores.append(pltpu.make_async_copy(o_ref.at[:, :, cols], o_hbm.at[:, :, cols], sem.at[c]))
        stores[-1].start()
    for store in stores:
        store.wait()


def unpack(q, kv, chunks=8):
    shape = (3, q.shape[1], HEADS * DH)
    vmem = pl.BlockSpec(memory_space=pltpu.VMEM)
    return pl.pallas_call(
        functools.partial(unpack_kernel, chunks),
        out_shape=jax.ShapeDtypeStruct(shape, BF16),
        in_specs=[vmem, vmem],
        out_specs=pl.BlockSpec(memory_space=pl.ANY),
        scratch_shapes=[pltpu.VMEM(shape, BF16), pltpu.SemaphoreType.DMA((chunks,))],
        compiler_params=pltpu.CompilerParams(vmem_limit_bytes=16 * MIB),
        name="unpack",
    )(q, kv)


def whole(shape):
    return pl.BlockSpec(shape, lambda i: (0,) * len(shape), pipeline_mode=pl.Buffered(1))


def scalars():
    return pl.BlockSpec(memory_space=pltpu.SMEM)


def dot(a, b):
    return jnp.dot(a, b, preferred_element_type=F32)


def dot_rows(a, b):
    return lax.dot_general(a, b, (((0,), (0,)), ((), ())), preferred_element_type=F32)


def token_rows(x_ref, plane, start, count):
    tok = x_ref.shape[2]
    return x_ref[pl.ds(start // tok, count // tok), plane].reshape(count, DH)


def live_rows(g, start, length):
    row = start + lax.broadcasted_iota(jnp.int32, g.shape, 0)
    return jnp.where(row < length, g, jnp.zeros_like(g))


def fold(x, op):
    return op(x.reshape(x.shape[0] // 8, 8, x.shape[1]), axis=0)


def mask_past(s, r0, offset):
    key = r0 + lax.broadcasted_iota(jnp.int32, s.shape, 0)
    return jnp.where(key < offset, s, NEG)


def past_copies(pk_hbm, pv_hbm, pk_ref, pv_ref, sems, b):
    rows = pl.ds(pl.multiple_of(b * BK, BK), BK)
    return (
        pltpu.make_async_copy(pk_hbm.at[rows], pk_ref.at[rows], sems.at[0, b]),
        pltpu.make_async_copy(pv_hbm.at[rows], pv_ref.at[rows], sems.at[1, b]),
    )


def each(count, action):
    def body(b, carry):
        action(b)
        return carry

    lax.fori_loop(0, count, body, 0)


def span_kernel(
    bounds, x_hbm, pk_hbm, pv_hbm, okv_ref, dq_ref, stat_ref,
    x_ref, pk_ref, pv_ref, s_sc, dp_sc, dka, dva, x_sem, past_sem,
):
    n, _, tok, _ = x_ref.shape
    i = pl.program_id(0)
    offset = bounds[0]
    length = bounds[1]
    qstart = i * BQ
    n_past = (offset + BK - 1) // BK

    def x_copy(c):
        rows = pl.ds(c * (BQ // tok), BQ // tok)
        return pltpu.make_async_copy(x_hbm.at[rows], x_ref.at[rows], x_sem.at[c])

    def start_past(b):
        for copy in past_copies(pk_hbm, pv_hbm, pk_ref, pv_ref, past_sem, b):
            copy.start()

    def wait_past(b):
        @pl.when(i == 0)
        def _():
            for copy in past_copies(pk_hbm, pv_hbm, pk_ref, pv_ref, past_sem, b):
                copy.wait()

    @pl.when(i == 0)
    def _():
        x_copy(0).start()
        each(n_past, start_past)
        for c in range(1, n * tok // BQ):
            x_copy(c).start()

    @pl.when(i == 0)
    def _():
        dka[...] = jnp.zeros_like(dka)
        dva[...] = jnp.zeros_like(dva)

    x_copy(i).wait()

    @pl.when(qstart >= length)
    def _():
        dq_ref[...] = jnp.zeros_like(dq_ref)
        stat_ref[...] = jnp.zeros_like(stat_ref)
        each(n_past, wait_past)

    @pl.when(qstart < length)
    def _():
        q = token_rows(x_ref, 0, qstart, BQ)
        g = live_rows(token_rows(x_ref, 3, qstart, BQ), qstart, length)
        q_t = q.T
        g_t = g.T
        half = BQ // 2
        lo = pl.ds(pl.multiple_of(qstart, BQ), half)
        hi = pl.ds(pl.multiple_of(qstart + half, half), half)

        def update(s, dp, carry):
            m, l, d = carry
            m_new = jnp.maximum(m, jnp.max(fold(s, jnp.max), axis=0, keepdims=True))
            keep = jnp.exp2((m - m_new) * SCALE_LOG2)
            e = jnp.exp2(s * SCALE_LOG2 - m_new * SCALE_LOG2)
            return m_new, l * keep + fold(e, jnp.sum), d * keep + fold(e * dp, jnp.sum)

        def past_stats(b, carry, masked):
            wait_past(b)
            r0 = pl.multiple_of(b * BK, BK)
            size = BK // 2
            parts = [pl.ds(r0 + k * size, size) for k in range(2)]
            s = [dot(pk_ref[r, :], q_t) for r in parts]
            dp = [dot(pv_ref[r, :], g_t) for r in parts]
            for k in range(2):
                if masked:
                    s[k] = mask_past(s[k], r0 + k * size, offset)
                carry = update(s[k], dp[k], carry)
            return carry

        def span_stats(b, carry):
            r0 = pl.multiple_of(b * BQ, BQ)
            s = dot(token_rows(x_ref, 1, r0, BQ), q_t)
            dp = dot(token_rows(x_ref, 2, r0, BQ), g_t)
            s_sc[pl.ds(r0, BQ), :] = s
            dp_sc[pl.ds(r0, BQ), :] = dp
            return update(s, dp, carry)

        def diagonal_stats(carry):
            key = lax.broadcasted_iota(jnp.int32, (half, BQ), 0)
            query = lax.broadcasted_iota(jnp.int32, (half, BQ), 1)
            s = dot(token_rows(x_ref, 1, qstart, half), q_t)
            dp = dot(token_rows(x_ref, 2, qstart, half), g_t)
            s_hi = dot(token_rows(x_ref, 1, qstart + half, half), q_t[:, half:])
            dp_hi = dot(token_rows(x_ref, 2, qstart + half, half), g_t[:, half:])
            s = jnp.where((key <= query) & (qstart + key < length), s, NEG)
            s_sc[lo, :] = s
            dp_sc[lo, :] = dp
            carry = update(s, dp, carry)
            key = key[:, :half]
            seen = (key <= query[:, :half]) & (qstart + half + key < length)
            s_hi = jnp.where(seen, s_hi, NEG)
            s_sc[hi, half:] = s_hi
            dp_sc[hi, half:] = dp_hi
            right = update(s_hi, dp_hi, tuple(c[:, half:] for c in carry))
            return tuple(jnp.concatenate([c[:, :half], r], axis=1) for c, r in zip(carry, right))

        zero = jnp.zeros((8, BQ), F32)
        carry = (jnp.full((1, BQ), NEG, F32), zero, zero)
        carry = lax.fori_loop(0, i, span_stats, carry)
        carry = diagonal_stats(carry)
        full = offset // BK
        carry = lax.fori_loop(0, full, functools.partial(past_stats, masked=False), carry)
        m, l, d = lax.fori_loop(
            full, n_past, functools.partial(past_stats, masked=True), carry
        )
        l = jnp.sum(l, axis=0, keepdims=True)
        delta = jnp.sum(d, axis=0, keepdims=True) / l
        lse = m * SCALE_LOG2 + jnp.log2(l)
        stat_ref[...] = jnp.concatenate([lse, delta, jnp.zeros((6, BQ), F32)], axis=0)

        def p_and_ds(rows, cols):
            p = jnp.exp2(s_sc[rows, cols] * SCALE_LOG2 - lse[:, cols])
            return p.astype(BF16), (p * (dp_sc[rows, cols] - delta[:, cols])).astype(BF16)

        def span_grads(b, dq):
            rows = pl.ds(pl.multiple_of(b * BQ, BQ), BQ)
            p, ds = p_and_ds(rows, slice(0, BQ))
            dva[rows, :] += dot(p, g)
            dka[rows, :] += dot(ds, q)
            return dq + dot_rows(ds, token_rows(x_ref, 1, b * BQ, BQ))

        dq = lax.fori_loop(0, i, span_grads, jnp.zeros((BQ, DH), F32))
        p, ds = p_and_ds(lo, slice(0, BQ))
        p_hi, ds_hi = p_and_ds(hi, slice(half, BQ))
        dva[lo, :] += dot(p, g)
        dka[lo, :] += dot(ds, q)
        dva[hi, :] += dot(p_hi, g[half:])
        dka[hi, :] += dot(ds_hi, q[half:])
        dq = dq + dot_rows(ds, token_rows(x_ref, 1, qstart, half))
        dq_ref[:half] = dq[:half]
        dq_ref[half:] = dq[half:] + dot_rows(ds_hi, token_rows(x_ref, 1, qstart + half, half))

    @pl.when(i == pl.num_programs(0) - 1)
    def _():
        okv_ref[:, 0] = (dka[...] * SCALE).astype(BF16).reshape(n, tok, DH)
        okv_ref[:, 1] = dva[...].astype(BF16).reshape(n, tok, DH)


def span_grads_and_stats(bounds, x, pk, pv):
    n, _, tok, _ = x.shape
    span = n * tok
    return pl.pallas_call(
        span_kernel,
        out_shape=(
            jax.ShapeDtypeStruct((n, 2, tok, DH), BF16),
            jax.ShapeDtypeStruct((span, DH), F32),
            jax.ShapeDtypeStruct((8, span), F32),
        ),
        grid_spec=pl.GridSpec(
            grid=(span // BQ,),
            in_specs=[scalars()] + [pl.BlockSpec(memory_space=pl.ANY)] * 3,
            out_specs=(
                whole((n, 2, tok, DH)),
                pl.BlockSpec((BQ, DH), lambda i: (i, 0)),
                pl.BlockSpec((8, BQ), lambda i: (0, i)),
            ),
            scratch_shapes=[
                pltpu.VMEM(x.shape, BF16),
                pltpu.VMEM(pk.shape, BF16),
                pltpu.VMEM(pv.shape, BF16),
                pltpu.VMEM((span, BQ), F32),
                pltpu.VMEM((span, BQ), F32),
                pltpu.VMEM((span, DH), F32),
                pltpu.VMEM((span, DH), F32),
                pltpu.SemaphoreType.DMA((span // BQ,)),
                pltpu.SemaphoreType.DMA((2, pk.shape[0] // BK)),
            ],
        ),
        compiler_params=pltpu.CompilerParams(vmem_limit_bytes=62 * MIB),
        cost_estimate=pl.CostEstimate(flops=7 * 10**9, bytes_accessed=6 * 10**6, transcendentals=10**7),
        name="attn_span",
    )(bounds, x, pk, pv)


def query_kernel(
    first, bounds, q_ref, g_ref, pk_hbm, pv_hbm, dqs_ref, stat_ref, o_ref, pk_ref, pv_ref, past_sem
):
    tok = q_ref.shape[2]
    i = pl.program_id(0)
    offset = bounds[0]
    length = bounds[1]
    qstart = (first + i) * BQ
    n_past = (offset + BK - 1) // BK

    def start_past(b):
        for copy in past_copies(pk_hbm, pv_hbm, pk_ref, pv_ref, past_sem, b):
            copy.start()

    def wait_past(b):
        @pl.when(i == 0)
        def _():
            for copy in past_copies(pk_hbm, pv_hbm, pk_ref, pv_ref, past_sem, b):
                copy.wait()

    @pl.when(i == 0)
    def _():
        each(n_past, start_past)

    @pl.when(qstart >= length)
    def _():
        o_ref[...] = jnp.zeros_like(o_ref)
        each(n_past, wait_past)

    @pl.when(qstart < length)
    def _():
        q_t = q_ref[:, 0].reshape(BQ, DH).T
        g_t = live_rows(g_ref[:, 0].reshape(BQ, DH), qstart, length).T
        lse = stat_ref[0:1]
        delta = stat_ref[1:2]

        def step(b, dq):
            wait_past(b)
            r0 = pl.multiple_of(b * BK, BK)
            keys = pk_ref[pl.ds(r0, BK), :]
            p = jnp.exp2(mask_past(dot(keys, q_t), r0, offset) * SCALE_LOG2 - lse)
            dp = dot(pv_ref[pl.ds(r0, BK), :], g_t)
            ds = (p * (dp - delta)).astype(BF16)
            return dq + dot_rows(ds, keys)

        dq = lax.fori_loop(0, n_past, step, dqs_ref[...])
        o_ref[...] = (dq * SCALE).astype(BF16).reshape(BQ // tok, tok, DH)


def query_grads(bounds, x, pk, pv, dq_span, stats, first, count):
    _, _, tok, _ = x.shape
    group = BQ // tok
    hbm = pl.BlockSpec(memory_space=pl.ANY)
    return pl.pallas_call(
        functools.partial(query_kernel, first),
        out_shape=jax.ShapeDtypeStruct((count * group, tok, DH), BF16),
        grid_spec=pl.GridSpec(
            grid=(count,),
            in_specs=[
                scalars(),
                pl.BlockSpec((group, 1, tok, DH), lambda i: (first + i, 0, 0, 0)),
                pl.BlockSpec((group, 1, tok, DH), lambda i: (first + i, 3, 0, 0)),
                hbm,
                hbm,
                pl.BlockSpec((BQ, DH), lambda i: (first + i, 0)),
                pl.BlockSpec((8, BQ), lambda i: (0, first + i)),
            ],
            out_specs=pl.BlockSpec((group, tok, DH), lambda i: (i, 0, 0)),
            scratch_shapes=[
                pltpu.VMEM(pk.shape, BF16),
                pltpu.VMEM(pv.shape, BF16),
                pltpu.SemaphoreType.DMA((2, pk.shape[0] // BK)),
            ],
        ),
        compiler_params=pltpu.CompilerParams(vmem_limit_bytes=62 * MIB),
        cost_estimate=pl.CostEstimate(
            flops=10**9 * count, bytes_accessed=10**6 * count, transcendentals=2 * 10**6 * count
        ),
    )(bounds, x, x, pk, pv, dq_span, stats)


def past_kernel(first, bounds, x_ref, pk_ref, pv_ref, stat_ref, acc_ref, prev_ref, nacc_ref, dk, dv):
    del prev_ref
    offset = bounds[0]
    length = bounds[1]
    kstart = (first + pl.program_id(0)) * PK
    dk[...] = jnp.zeros_like(dk)
    dv[...] = jnp.zeros_like(dv)

    def step(i, carry):
        qstart = pl.multiple_of(i * BQ, BQ)
        q = token_rows(x_ref, 0, qstart, BQ)
        g = live_rows(token_rows(x_ref, 3, qstart, BQ), qstart, length)
        s = mask_past(dot(pk_ref[...], q.T), kstart, offset)
        p = jnp.exp2(s * SCALE_LOG2 - stat_ref[0:1, pl.ds(qstart, BQ)])
        dp = dot(pv_ref[...], g.T)
        ds = (p * (dp - stat_ref[1:2, pl.ds(qstart, BQ)])).astype(BF16)
        dk[...] += dot(ds, q)
        dv[...] += dot(p.astype(BF16), g)
        return carry

    @pl.when(kstart < offset)
    def _():
        lax.fori_loop(0, (length + BQ - 1) // BQ, step, 0)

    even = pl.ds(0, PK, stride=2)
    odd = pl.ds(1, PK, stride=2)
    nacc_ref[even, :] = acc_ref[even, :] + dk[...] * SCALE
    nacc_ref[odd, :] = acc_ref[odd, :] + dv[...]


def past_grads(bounds, x, pk, pv, stats, accum, first, count, prev=None):
    keys = pl.BlockSpec((PK, DH), lambda i: (first + i, 0))
    pairs = pl.BlockSpec((2 * PK, DH), lambda i: (first + i, 0))
    args = [bounds, x, pk, pv, stats, accum]
    in_specs = [scalars(), whole(x.shape), keys, keys, whole(stats.shape), pairs]
    body = functools.partial(past_kernel, first)
    aliases = {}
    if prev is None:
        body = lambda *refs: past_kernel(first, *refs[:6], None, *refs[6:])
    else:
        args.append(prev)
        in_specs.append(pl.BlockSpec(memory_space=pl.ANY))
        aliases = {6: 0}
    return pl.pallas_call(
        body,
        out_shape=jax.ShapeDtypeStruct(accum.shape, F32),
        grid_spec=pl.GridSpec(
            grid=(count,),
            in_specs=in_specs,
            out_specs=pairs,
            scratch_shapes=[pltpu.VMEM((PK, DH), F32), pltpu.VMEM((PK, DH), F32)],
        ),
        input_output_aliases=aliases,
        compiler_params=pltpu.CompilerParams(vmem_limit_bytes=62 * MIB),
        cost_estimate=pl.CostEstimate(
            flops=2 * 10**9 * count, bytes_accessed=4 * 10**6 * count, transcendentals=10**6 * count
        ),
    )(*args)


def to_heads(x):
    return lax.all_to_all(x, "seq", split_axis=0, concat_axis=0, tiled=True)


def from_behind(block, axis, distance):
    size = lax.axis_size(axis)
    return lax.ppermute(block, axis, [((i - distance) % size, i) for i in range(size)])


def per_device(span_inputs, out_grad, past_cache, past_accum, offsets, lengths):
    past = past_cache.shape[1]
    bounds = jnp.concatenate([offsets, lengths])
    cache = past_cache.reshape(past, 2, DH)
    pk, pv = cache[:, 0], cache[:, 1]
    x = to_heads(pack(jnp.transpose(span_inputs[0], (1, 0, 2)), out_grad[0]))
    kv, dq_span, stats = span_grads_and_stats(bounds, x, pk, pv)
    kv = to_heads(kv)
    half = x.shape[0] * x.shape[2] // BQ // 2
    low = query_grads(bounds, x, pk, pv, dq_span, stats, 0, half)
    low, bounds = lax.optimization_barrier((low, bounds))
    low = from_behind(low, "section", -1)
    high = query_grads(bounds, x, pk, pv, dq_span, stats, half, half)
    high, bounds = lax.optimization_barrier((high, bounds))
    high = from_behind(high, "section", -1)
    accum = past_accum.reshape(past * 2, DH)
    new_accum = past_grads(bounds, x, pk, pv, stats, accum, 0, 1)
    kv, dq, new_accum, bounds = lax.optimization_barrier(
        (kv, jnp.concatenate([low, high]), new_accum, bounds)
    )
    dq = to_heads(dq)
    kv = from_behind(kv, "section", -1)
    new_accum = past_grads(bounds, x, pk, pv, stats, accum, 1, past // PK - 1, new_accum)
    out = jnp.transpose(unpack(dq, kv), (1, 0, 2))
    return out[None], new_accum.reshape(past_accum.shape)


def solution(mesh):
    in_specs = (
        P("section", "seq", None, None),
        P("section", "seq", None),
        P("section", None, None, "seq", None),
        P("section", None, None, "seq", None),
        P("section"),
        P("section"),
    )
    out_specs = (P("section", "seq", None, None), P("section", None, None, "seq", None))
    return jax.shard_map(
        per_device, mesh=mesh, in_specs=in_specs, out_specs=out_specs, check_vma=False
    )
```
